128 devices in a mesh: tile: 16 (over y, z), depth: 8 (over x, core).
Axes of the slice: x: 4, y: 4, z: 4, core: 2. Of those that a mesh axis runs over, the one named last changes fastest.
Arguments:
- owned_blocks: bfloat16 [8, 1024, 32768], P('depth', 'tile'), may hold values from -6 to 6
- slot_counts: int32 [8, 16], P('depth'), may hold values from 1 to 64, 512 in all within a row
- brick_order: int32 [8, 16], P('depth'), may hold values from 0 to 15, each once within a row
- view_flip: int32 [16], replicated, may hold values from 0 to 1
- tf_centers: float32 [8], replicated, may hold values from -2.5 to 2.5
- tf_amps: float32 [4, 8], replicated, may hold values from -6 to 6
Outputs:
- image: float32 [4, 128, 2048], P(None, 'depth', 'tile')
The draws below stay inside these ranges and needn't reach their ends.
Inputs may be any that keep to these rules, and one draw needn't show every extreme that they name: `slot_counts`: every row sums to 512, and some entry of every row equals 64. `brick_order`: every row holds each of 0 to 15 once.
All inputs are finite; a program needn't handle non-finite values.
Results may differ from the reference program's by a relative error of at most 0.0003.
Values may be sent and summed in bfloat16 or wider, within the bound.
A program may use at most 64 MiB of HBM per device.

```python
import math
import jax
import jax.numpy as jnp
import numpy as np

BLOCK = 32
BX = 4
BY = 4
DB = 2
KNOTS = 8
BRICK_BLOCKS = 32
SLOTS = 64
CELLS = 32768
NX = 2048
NY = 128
NZ = 512
N_TILE = 16
N_DEPTH = 8


def touch_ends(values, stream_key, smallest, largest):
    extent = values.shape
    index_at = [jax.random.randint(jax.random.fold_in(stream_key, axis), (), 0, extent[axis]) for axis in range(len(extent))]
    values = values.at[tuple(index_at)].set(smallest)
    longest = extent.index(max(extent))
    index_at[longest] = (index_at[longest] + 1) % extent[longest]
    return values.at[tuple(index_at)].set(largest)


def block_scale(own_key, dims, shards, low, top_value):
    def one(dim, parts):
        steps = jax.random.uniform(jax.random.fold_in(jax.random.fold_in(own_key, 6), dim), (parts,), jnp.float32, low / len(shards), top_value / len(shards))
        return jnp.repeat(jnp.exp(steps), dims[dim] // parts).reshape((-1,) + (1,) * (len(dims) - dim - 1))

    loudness = one(*shards[0])
    for cut in shards[1:]:
        loudness = loudness * one(*cut)
    return loudness


def profile(number_of, total, reach, slope):
    loads = [(1 << 20) // math.isqrt(grade ** slope) + 1 for grade in range(2, number_of + 1)]
    rest, given = total - reach - (number_of - 1), [1] * (number_of - 1)
    while rest > 0:
        movable = [i for i in range(number_of - 1) if given[i] < reach]
        mass, remaining = sum([loads[i] for i in movable]), rest
        for i in movable:
            addition = min(reach - given[i], max(1, remaining * loads[i] // mass), rest)
            given[i] = given[i] + addition
            rest = rest - addition
    return np.array([reach] + given)


def ragged(key, number_of, total, most, slope):
    if number_of == 2:
        one = jax.random.randint(key, (), max(1, total - most), min(most, total - 1) + 1)
        return jnp.stack([one, total - one])
    tallies = jnp.asarray(profile(number_of, total, most, slope), jnp.int32)
    couples = (number_of - 1) // 2
    giver, receiver = tallies[1:1 + 2 * couples:2], tallies[2:2 + 2 * couples:2]
    margin = jnp.minimum(giver - 1, most - receiver)
    moved = jax.random.randint(jax.random.fold_in(key, 1), (couples,), 0, 1 << 20) % (margin + 1)
    tallies = tallies.at[1:1 + 2 * couples:2].set(giver - moved).at[2:2 + 2 * couples:2].set(receiver + moved)
    return tallies[jax.random.permutation(jax.random.fold_in(key, 2), number_of)]


def gaussian(key, dims, deviation, most, pieces=(), kind=jnp.bfloat16):
    drawn = jax.random.normal(key, dims, jnp.float32) * deviation
    if len(pieces) > 0:
        drawn = block_scale(key, dims, pieces, -0.22, 0.18) * drawn
    return jnp.clip(drawn, min=-most, max=most).astype(kind)


def setup_inputs(seed: int = 0) -> dict:
    streams_of = jax.random.split(jax.random.key(seed), 7)
    return {
        "owned_blocks": gaussian(streams_of[0], (N_DEPTH, N_TILE * SLOTS, CELLS), 1.0, 6.0, ((0, 8), (1, 16))),
        "slot_counts": jax.vmap(lambda own: ragged(own, N_TILE, N_TILE * BRICK_BLOCKS, SLOTS, 2))(jax.random.split(streams_of[1], N_DEPTH)).reshape((N_DEPTH, N_TILE)).astype(jnp.int32),
        "brick_order": jax.vmap(lambda own: jax.random.permutation(own, N_TILE))(jax.random.split(streams_of[2], N_DEPTH)).reshape((N_DEPTH, N_TILE)).astype(jnp.int32),
        "view_flip": touch_ends(jax.random.randint(streams_of[3], (N_TILE,), 0, 2), jax.random.fold_in(streams_of[3], 1), 0, 1).astype(jnp.int32),
        "tf_centers": jnp.clip(jax.random.uniform(streams_of[4], (KNOTS,), jnp.float32, -2.5, 2.5), -2.5, 2.5),
        "tf_amps": gaussian(streams_of[5], (4, KNOTS), 1.5, 6.0, (), jnp.float32),
    }


bump_scale = 4.0


def over_blend(nearer, farther):
    return nearer + (1.0 - nearer[3:4]) * farther


def reference(owned_blocks, slot_counts, brick_order, view_flip, tf_centers, tf_amps):
    step_size = 1.5 / NZ
    brick_total = BX * BY * DB
    tile_lane = jnp.arange(N_TILE, dtype=jnp.int32)
    flip_column = jnp.repeat(view_flip, BX * BLOCK)
    partials = []
    for depth_row in range(N_DEPTH):
        counts = slot_counts[depth_row].astype(jnp.int32)
        order_row = brick_order[depth_row].astype(jnp.int32)
        starts = (jnp.cumsum(counts) - counts).astype(jnp.int32)
        position = jnp.sum(jnp.where(order_row[None, :] == tile_lane[:, None], tile_lane[None, :], 0), axis=1).astype(jnp.int32)
        local_index = jnp.arange(brick_total, dtype=jnp.int32)
        wanted = (local_index[None, :] * N_TILE + position[:, None]).astype(jnp.int32)
        owner_index = (jnp.sum((starts[None, None, :] <= wanted[:, :, None]).astype(jnp.int32), axis=2) - 1).astype(jnp.int32)
        slot_index = (owner_index * SLOTS + wanted - starts[owner_index]).astype(jnp.int32)
        blocks = owned_blocks[depth_row][slot_index.reshape(-1)]
        volume = blocks.reshape(N_TILE, DB, BY, BX, BLOCK, BLOCK, BLOCK).transpose(1, 4, 2, 5, 0, 3, 6)
        values = volume.reshape(DB * BLOCK, NY, NX).astype(jnp.float32)
        fields = [jnp.zeros_like(values) for channel in range(4)]
        for knot_index in range(KNOTS):
            bump_term = jnp.exp(-bump_scale * jnp.square(values - tf_centers[knot_index]))
            fields = [fields[channel] + tf_amps[channel, knot_index] * bump_term for channel in range(4)]
        extinction = jax.nn.softplus(fields[3])
        opacity_step = 1.0 - jnp.exp(-step_size * extinction)
        running = jnp.cumsum(extinction, axis=0)
        total = jnp.sum(extinction, axis=0)
        before = jnp.where(flip_column[None, None, :] == 1, total[None] - running, running - extinction)
        passed = jnp.exp(-step_size * before) * opacity_step
        colors = [jnp.sum(passed * jax.nn.sigmoid(fields[channel]), axis=0) for channel in range(3)]
        opacity = 1.0 - jnp.exp(-step_size * total)
        partials.append(jnp.stack(colors + [opacity], axis=0))
    rising = jnp.zeros((4, NY, NX), jnp.float32)
    for level_index in range(N_DEPTH - 1, -1, -1):
        rising = over_blend(partials[level_index], rising)
    falling = jnp.zeros((4, NY, NX), jnp.float32)
    for level_index in range(N_DEPTH):
        falling = over_blend(partials[level_index], falling)
    return jnp.where(flip_column[None, None, :] == 1, falling, rising)
```

```python
import functools

import jax
import jax.numpy as jnp
from jax import lax
from jax.experimental import pallas as pl
from jax.experimental.pallas import tpu as pltpu
from jax.sharding import PartitionSpec as P

MESH = pl.DeviceIdType.MESH
BLOCK = 32
KNOTS = 8
N_TILE = 16
N_DEPTH = 8
GROUPS = 4
LANES = 128
PIXELS = BLOCK * BLOCK
CHUNKS = PIXELS // LANES
STEP = 1.5 / 512


def march(vox, img, sign, row0, chunk, centers, amps):
    step_sign = sign * STEP

    def body(z, carry):
        total, held, red, green, blue = carry
        lane = pl.multiple_of(z * PIXELS + chunk * LANES, LANES)
        value = vox[pl.ds(row0, N_TILE), pl.ds(lane, LANES)].astype(jnp.float32)
        fields = [None] * 4
        for k in range(KNOTS):
            off = value - centers[k]
            bump = jnp.exp(off * off * -4.0)
            for c in range(4):
                term = amps[c][k] * bump
                fields[c] = term if k == 0 else fields[c] + term
        total = total + jnp.log(1.0 + jnp.exp(fields[3]))
        now = jnp.exp(total * step_sign)
        weight = held - now
        red = red + weight * jnp.tanh(fields[0])
        green = green + weight * jnp.tanh(fields[1])
        blue = blue + weight * jnp.tanh(fields[2])
        return total, now, red, green, blue

    zero = jnp.zeros((N_TILE, LANES), jnp.float32)
    total, held, red, green, blue = lax.fori_loop(
        0, BLOCK, body, (zero, zero + 1.0, zero, zero, zero), unroll=4
    )
    through = jnp.exp(total * -STEP)
    scale = jnp.where(sign < 0.0, 0.5, -0.5 * through)
    half = chunk // 4
    quarter = chunk % 4
    for c, colour in enumerate((red, green, blue)):
        img[half * 16 + c * 4 + quarter] = scale * ((1.0 - held) + colour)
    img[half * 16 + 12 + quarter] = 1.0 - through


def over(nearer, farther):
    low, high = nearer[0:8], nearer[8:16]
    clear = 1.0 - high
    clear = jnp.concatenate([clear[4:8], clear[4:8]], axis=0)
    return jnp.concatenate([low + clear * farther[0:8], high + clear * farther[8:16]], axis=0)


def render(
    counts, order, flips, centers_ref, amps_ref, blocks, out,
    vox, img, send, recv, dsend, drecv, starts, rows, found,
    load_sem, send_sem, recv_sem, dsend_sem, drecv_sem,
):
    me = lax.axis_index("tile")
    my_depth = lax.axis_index("depth")
    loads = []
    for m in range(GROUPS):
        part = pl.ds(m * N_TILE, N_TILE)
        load = pltpu.make_async_copy(blocks.at[part, :], vox.at[part, :], load_sem.at[m])
        load.start()
        loads.append(load)
    barrier = pltpu.get_barrier_semaphore()
    for o in range(1, N_TILE):
        pl.semaphore_signal(
            barrier, inc=1, device_id={"tile": (me + o) % N_TILE}, device_id_type=MESH
        )
    for o in range(1, N_DEPTH):
        pl.semaphore_signal(
            barrier, inc=1, device_id={"depth": (my_depth + o) % N_DEPTH}, device_id_type=MESH
        )

    running = jnp.int32(0)
    my_start = jnp.int32(0)
    my_position = jnp.int32(0)
    start_list = []
    for i in range(N_TILE):
        start_list.append(running)
        my_start = jnp.where(me == i, running, my_start)
        my_position = jnp.where(order[i] == me, i, my_position)
        running = running + counts[i]
    for o in range(N_TILE):
        tile = (me + o) % N_TILE
        position = jnp.int32(0)
        for i in range(N_TILE):
            position = jnp.where(order[i] == tile, i, position)
        rows[o] = (position - my_start) & (N_TILE - 1)

    def find(index, carry):
        wanted = index * N_TILE + my_position
        owner = jnp.int32(0)
        first = jnp.int32(0)
        for i in range(1, N_TILE):
            past = start_list[i] <= wanted
            owner = jnp.where(past, i, owner)
            first = jnp.where(past, start_list[i], first)
        found[index] = (((wanted - first) >> 4) & (GROUPS - 1)) * N_TILE + owner
        return carry

    lax.fori_loop(0, 2 * N_TILE, find, 0)
    my_flip = flips[me]
    slot = lax.broadcasted_iota(jnp.int32, (N_TILE, LANES), 0)
    sign = jnp.full((N_TILE, LANES), -1.0, jnp.float32)
    for s in range(N_TILE):
        flip = flips[order[(my_start + s) & (N_TILE - 1)]].astype(jnp.float32)
        sign = jnp.where(slot == s, 2.0 * flip - 1.0, sign)
    centers = [centers_ref[k] for k in range(KNOTS)]
    amps = [[amps_ref[c, k] * (1.0 if c == 3 else 0.5) for k in range(KNOTS)] for c in range(4)]

    def exchange(m, o):
        return pltpu.make_async_remote_copy(
            src_ref=send.at[m, o],
            dst_ref=recv.at[m * N_TILE + me],
            send_sem=send_sem.at[m, o],
            recv_sem=recv_sem.at[m, o],
            device_id={"tile": (me + o) % N_TILE},
            device_id_type=MESH,
        )

    copies = []
    for m in range(GROUPS):
        loads[m].wait()

        def column(chunk, carry):
            march(vox, img, sign, m * N_TILE, chunk, centers, amps)
            return carry

        lax.fori_loop(0, CHUNKS, column, 0)
        for o in range(N_TILE):
            image = img[:, rows[o], :]
            if o == 0:
                recv[m * N_TILE + me] = image
            else:
                send[m, o] = image
        if m == 0:
            pl.semaphore_wait(barrier, N_TILE + N_DEPTH - 2)
        for o in range(1, N_TILE):
            copy = exchange(m, o)
            copy.start()
            copies.append(copy)
    for copy in copies:
        copy.wait_recv()

    def layered(depth):
        by = depth // 2
        half = depth % 2
        parts = []
        for bx in range(4):
            low = found[by * 4 + bx]
            high = found[16 + by * 4 + bx]
            near = recv[jnp.where(my_flip == 1, high, low), pl.ds(half * 16, 16), :]
            far = recv[jnp.where(my_flip == 1, low, high), pl.ds(half * 16, 16), :]
            parts.append(over(near, far))
        return jnp.concatenate(parts, axis=0)

    shares = []
    for o in range(1, N_DEPTH):
        depth = (my_depth + o) % N_DEPTH
        dsend[o] = layered(depth)
        share = pltpu.make_async_remote_copy(
            src_ref=dsend.at[o],
            dst_ref=drecv.at[my_depth],
            send_sem=dsend_sem.at[o],
            recv_sem=drecv_sem.at[o],
            device_id={"depth": depth},
            device_id_type=MESH,
        )
        share.start()
        shares.append(share)
    drecv[my_depth] = layered(my_depth)
    for share in shares:
        share.wait_recv()

    blended = [jnp.zeros((16, LANES), jnp.float32) for bx in range(4)]
    for i in range(N_DEPTH):
        level = jnp.where(my_flip == 1, i, N_DEPTH - 1 - i)
        layer = drecv[level]
        blended = [over(layer[bx * 16 : bx * 16 + 16], blended[bx]) for bx in range(4)]
    lane_block = lax.broadcasted_iota(jnp.int32, (16, LANES), 1) // BLOCK
    for y in range(4):
        line = blended[0]
        for bx in range(4):
            shift = (bx - y) * BLOCK % LANES
            moved = pltpu.roll(blended[bx], shift, 1) if shift else blended[bx]
            line = moved if bx == 0 else jnp.where(lane_block == bx, moved, line)
        out[pl.ds(y, 16, stride=4), :] = line
    for copy in copies:
        copy.wait_send()
    for share in shares:
        share.wait_send()


def body(owned_blocks, slot_counts, brick_order, view_flip, tf_centers, tf_amps):
    smem = pl.BlockSpec(memory_space=pltpu.SMEM)
    image = pl.pallas_call(
        render,
        out_shape=jax.ShapeDtypeStruct((64, LANES), jnp.float32),
        in_specs=[smem] * 5 + [pl.BlockSpec(memory_space=pltpu.HBM)],
        out_specs=pl.BlockSpec(memory_space=pltpu.VMEM),
        scratch_shapes=[
            pltpu.VMEM((64, 32768), jnp.bfloat16),
            pltpu.VMEM((32, N_TILE, LANES), jnp.float32),
            pltpu.VMEM((GROUPS, N_TILE, 32, LANES), jnp.float32),
            pltpu.VMEM((64, 32, LANES), jnp.float32),
            pltpu.VMEM((N_DEPTH, 64, LANES), jnp.float32),
            pltpu.VMEM((N_DEPTH, 64, LANES), jnp.float32),
            pltpu.SMEM((N_TILE,), jnp.int32),
            pltpu.SMEM((N_TILE,), jnp.int32),
            pltpu.SMEM((2 * N_TILE,), jnp.int32),
            pltpu.SemaphoreType.DMA((GROUPS,)),
            pltpu.SemaphoreType.DMA((GROUPS, N_TILE)),
            pltpu.SemaphoreType.DMA((GROUPS, N_TILE)),
            pltpu.SemaphoreType.DMA((N_DEPTH,)),
            pltpu.SemaphoreType.DMA((N_DEPTH,)),
        ],
        compiler_params=pltpu.CompilerParams(
            collective_id=0, has_side_effects=True, vmem_limit_bytes=64000 * 1024
        ),
        name="render",
    )(
        slot_counts.reshape(N_TILE),
        brick_order.reshape(N_TILE),
        view_flip,
        tf_centers,
        tf_amps,
        owned_blocks.reshape(64, 32768),
    )
    return image.reshape(4, 16, LANES)


def solution(mesh):
    in_specs = (P("depth", "tile", None), P("depth", None), P("depth", None), P(), P(), P())
    out_specs = P(None, "depth", "tile")
    return jax.shard_map(body, mesh=mesh, in_specs=in_specs, out_specs=out_specs, check_vma=False)
```

```python
import functools

import jax
import jax.numpy as jnp
from jax import lax
from jax.experimental import pallas as pl
from jax.experimental.pallas import tpu as pltpu
from jax.sharding import PartitionSpec as P

MESH = pl.DeviceIdType.MESH
BLOCK = 32
KNOTS = 8
N_TILE = 16
N_DEPTH = 8
GROUPS = 4
LANES = 128
PIXELS = BLOCK * BLOCK
CHUNKS = PIXELS // LANES
STEP = 1.5 / 512
HALF = 8
WIDE = 256
LOG2E = 1.4426950408889634
SPAN = 4
SPANS = BLOCK // SPAN
PAIRS = PIXELS // WIDE


def split(x):
    high = x.astype(jnp.bfloat16)
    return high, x - high.astype(jnp.float32)


def set_mix(mix, centers, amps):
    row = lax.broadcasted_iota(jnp.int32, (HALF, KNOTS * HALF), 0)
    column = lax.broadcasted_iota(jnp.int32, (HALF, KNOTS * HALF), 1)
    same = column % HALF == row
    block = column // HALF
    center = jnp.zeros(row.shape, jnp.float32)
    for k in range(KNOTS):
        center = jnp.where(block == k, centers[k], center)
    fall = jnp.exp(center * center * -4.0)
    for c in range(4):
        value = jnp.zeros(row.shape, jnp.float32)
        for k in range(KNOTS):
            value = jnp.where(block == k, amps[c][k], value)
        value = jnp.where(same, value * fall * (LOG2E if c == 3 else 0.5), 0.0)
        high, rest = split(value)
        parts = [high.astype(jnp.float32)] * 2 + [rest]
        mix[c * HALF : (c + 1) * HALF, :] = jnp.concatenate(parts, axis=1).astype(jnp.bfloat16)


def set_fields(vox, mix, fields, slopes, index):
    index = jnp.minimum(index, GROUPS * PAIRS * SPANS - 1)
    row = pl.multiple_of(index // (PAIRS * SPANS) * N_TILE, N_TILE)
    first = index % SPANS * (SPAN * PIXELS) + index // SPANS % PAIRS * WIDE
    for u in range(SPAN):
        lane = pl.multiple_of(first + u * PIXELS, WIDE)
        both = vox[pl.ds(row, N_TILE), pl.ds(lane, WIDE)].astype(jnp.float32)
        for h in range(2):
            value = both[h * HALF : (h + 1) * HALF]
            slope = value * (4.0 * LOG2E)
            bump = jnp.concatenate([jnp.exp2(value * (s - slope)) for s in slopes], axis=0)
            high, rest = split(bump)
            parts = jnp.concatenate([high, rest.astype(jnp.bfloat16), high], axis=0)
            fields[u, h] = jnp.dot(mix[...], parts, preferred_element_type=jnp.float32)


def advance(fields, step_sign, carry):
    for u in range(SPAN):
        total, held, red, green, blue = carry
        field = [
            jnp.concatenate([fields[u, h, c * HALF : (c + 1) * HALF] for h in range(2)], axis=0)
            for c in range(4)
        ]
        total = total + jnp.log(1.0 + jnp.exp2(field[3]))
        now = jnp.exp2(total * step_sign)
        weight = held - now
        red = red + weight * jnp.tanh(field[0])
        green = green + weight * jnp.tanh(field[1])
        blue = blue + weight * jnp.tanh(field[2])
        carry = total, now, red, green, blue
    return carry


def march(vox, img, mix, even, odd, slopes, sign, group, pair):
    step_sign = sign * (STEP * LOG2E)
    base = (group * PAIRS + pair) * SPANS

    def body(i, carry):
        set_fields(vox, mix, odd, slopes, base + 2 * i + 1)
        carry = advance(even, step_sign, carry)
        set_fields(vox, mix, even, slopes, base + 2 * i + 2)
        return advance(odd, step_sign, carry)

    zero = jnp.zeros((N_TILE, WIDE), jnp.float32)
    total, held, red, green, blue = lax.fori_loop(
        0, SPANS // 2, body, (zero, zero + 1.0, zero, zero, zero)
    )
    through = jnp.exp2(total * (-STEP * LOG2E))
    scale = jnp.where(sign < 0.0, 0.5, -0.5 * through)
    values = [scale * ((1.0 - held) + colour) for colour in (red, green, blue)]
    values.append(1.0 - through)
    half = pair // 2
    for c in range(4):
        for side in range(2):
            quarter = pair % 2 * 2 + side
            row = pl.multiple_of((half * 16 + c * 4 + quarter) * N_TILE, N_TILE)
            img[pl.ds(row, N_TILE), :] = values[c][:, side * LANES : (side + 1) * LANES]


def over(nearer, farther):
    low, high = nearer[0:8], nearer[8:16]
    clear = 1.0 - high
    clear = jnp.concatenate([clear[4:8], clear[4:8]], axis=0)
    return jnp.concatenate([low + clear * farther[0:8], high + clear * farther[8:16]], axis=0)


def render(
    counts, order, flips, centers_ref, amps_ref, blocks, out,
    vox, img, mix, even, odd, send, recv, dsend, drecv, starts, rows, found,
    load_sem, send_sem, recv_sem, dsend_sem, drecv_sem,
):
    me = lax.axis_index("tile")
    my_depth = lax.axis_index("depth")
    loads = []
    for m in range(GROUPS):
        part = pl.ds(m * N_TILE, N_TILE)
        load = pltpu.make_async_copy(blocks.at[part, :], vox.at[part, :], load_sem.at[m])
        load.start()
        loads.append(load)
    barrier = pltpu.get_barrier_semaphore()
    for o in range(1, N_TILE):
        pl.semaphore_signal(
            barrier, inc=1, device_id={"tile": (me + o) % N_TILE}, device_id_type=MESH
        )
    for o in range(1, N_DEPTH):
        pl.semaphore_signal(
            barrier, inc=1, device_id={"depth": (my_depth + o) % N_DEPTH}, device_id_type=MESH
        )

    running = jnp.int32(0)
    my_start = jnp.int32(0)
    my_position = jnp.int32(0)
    start_list = []
    for i in range(N_TILE):
        start_list.append(running)
        my_start = jnp.where(me == i, running, my_start)
        my_position = jnp.where(order[i] == me, i, my_position)
        running = running + counts[i]
    for o in range(N_TILE):
        tile = (me + o) % N_TILE
        position = jnp.int32(0)
        for i in range(N_TILE):
            position = jnp.where(order[i] == tile, i, position)
        rows[o] = (position - my_start) & (N_TILE - 1)

    def find(index, carry):
        wanted = index * N_TILE + my_position
        owner = jnp.int32(0)
        first = jnp.int32(0)
        for i in range(1, N_TILE):
            past = start_list[i] <= wanted
            owner = jnp.where(past, i, owner)
            first = jnp.where(past, start_list[i], first)
        found[index] = (((wanted - first) >> 4) & (GROUPS - 1)) * N_TILE + owner
        return carry

    lax.fori_loop(0, 2 * N_TILE, find, 0)
    my_flip = flips[me]
    slot = lax.broadcasted_iota(jnp.int32, (N_TILE, WIDE), 0)
    sign = jnp.full((N_TILE, WIDE), -1.0, jnp.float32)
    for s in range(N_TILE):
        flip = flips[order[(my_start + s) & (N_TILE - 1)]].astype(jnp.float32)
        sign = jnp.where(slot == s, 2.0 * flip - 1.0, sign)
    centers = [centers_ref[k] for k in range(KNOTS)]
    amps = [[amps_ref[c, k] for k in range(KNOTS)] for c in range(4)]
    set_mix(mix, centers, amps)
    slopes = [center * (8.0 * LOG2E) for center in centers]

    def exchange(m, o):
        return pltpu.make_async_remote_copy(
            src_ref=send.at[m, o],
            dst_ref=recv.at[m * N_TILE + me],
            send_sem=send_sem.at[m, o],
            recv_sem=recv_sem.at[m, o],
            device_id={"tile": (me + o) % N_TILE},
            device_id_type=MESH,
        )

    copies = []
    for m in range(GROUPS):
        if m == 0:
            loads[0].wait()
            set_fields(vox, mix, even, slopes, 0)

        def column(pair, carry):
            if m + 1 < GROUPS:

                @pl.when(pair == PAIRS - 1)
                def _():
                    loads[m + 1].wait()

            march(vox, img, mix, even, odd, slopes, sign, m, pair)
            return carry

        lax.fori_loop(0, PAIRS, column, 0)
        for o in range(N_TILE):
            image = img[pl.ds(rows[o], 32, stride=N_TILE), :]
            if o == 0:
                recv[m * N_TILE + me] = image
            else:
                send[m, o] = image
        if m == 0:
            pl.semaphore_wait(barrier, N_TILE + N_DEPTH - 2)
        for o in range(1, N_TILE):
            copy = exchange(m, o)
            copy.start()
            copies.append(copy)
    for copy in copies:
        copy.wait_recv()

    def layered(depth):
        by = depth // 2
        half = depth % 2
        parts = []
        for bx in range(4):
            low = found[by * 4 + bx]
            high = found[16 + by * 4 + bx]
            near = recv[jnp.where(my_flip == 1, high, low), pl.ds(half * 16, 16), :]
            far = recv[jnp.where(my_flip == 1, low, high), pl.ds(half * 16, 16), :]
            parts.append(over(near, far))
        return jnp.concatenate(parts, axis=0)

    shares = []
    for o in range(1, N_DEPTH):
        depth = (my_depth + o) % N_DEPTH
        dsend[o] = layered(depth)
        share = pltpu.make_async_remote_copy(
            src_ref=dsend.at[o],
            dst_ref=drecv.at[my_depth],
            send_sem=dsend_sem.at[o],
            recv_sem=drecv_sem.at[o],
            device_id={"depth": depth},
            device_id_type=MESH,
        )
        share.start()
        shares.append(share)
    drecv[my_depth] = layered(my_depth)
    for share in shares:
        share.wait_recv()

    blended = [jnp.zeros((16, LANES), jnp.float32) for bx in range(4)]
    for i in range(N_DEPTH):
        level = jnp.where(my_flip == 1, i, N_DEPTH - 1 - i)
        layer = drecv[level]
        blended = [over(layer[bx * 16 : bx * 16 + 16], blended[bx]) for bx in range(4)]
    lane_block = lax.broadcasted_iota(jnp.int32, (16, LANES), 1) // BLOCK
    for y in range(4):
        line = blended[0]
        for bx in range(4):
            shift = (bx - y) * BLOCK % LANES
            moved = pltpu.roll(blended[bx], shift, 1) if shift else blended[bx]
            line = moved if bx == 0 else jnp.where(lane_block == bx, moved, line)
        out[pl.ds(y, 16, stride=4), :] = line
    for copy in copies:
        copy.wait_send()
    for share in shares:
        share.wait_send()


def body(owned_blocks, slot_counts, brick_order, view_flip, tf_centers, tf_amps):
    smem = pl.BlockSpec(memory_space=pltpu.SMEM)
    image = pl.pallas_call(
        render,
        out_shape=jax.ShapeDtypeStruct((64, LANES), jnp.float32),
        in_specs=[smem] * 5 + [pl.BlockSpec(memory_space=pltpu.HBM)],
        out_specs=pl.BlockSpec(memory_space=pltpu.VMEM),
        scratch_shapes=[
            pltpu.VMEM((64, 32768), jnp.bfloat16),
            pltpu.VMEM((32 * N_TILE, LANES), jnp.float32),
            pltpu.VMEM((4 * HALF, 3 * KNOTS * HALF), jnp.bfloat16),
            pltpu.VMEM((SPAN, 2, 4 * HALF, WIDE), jnp.float32),
            pltpu.VMEM((SPAN, 2, 4 * HALF, WIDE), jnp.float32),
            pltpu.VMEM((GROUPS, N_TILE, 32, LANES), jnp.float32),
            pltpu.VMEM((64, 32, LANES), jnp.float32),
            pltpu.VMEM((N_DEPTH, 64, LANES), jnp.float32),
            pltpu.VMEM((N_DEPTH, 64, LANES), jnp.float32),
            pltpu.SMEM((N_TILE,), jnp.int32),
            pltpu.SMEM((N_TILE,), jnp.int32),
            pltpu.SMEM((2 * N_TILE,), jnp.int32),
            pltpu.SemaphoreType.DMA((GROUPS,)),
            pltpu.SemaphoreType.DMA((GROUPS, N_TILE)),
            pltpu.SemaphoreType.DMA((GROUPS, N_TILE)),
            pltpu.SemaphoreType.DMA((N_DEPTH,)),
            pltpu.SemaphoreType.DMA((N_DEPTH,)),
        ],
        compiler_params=pltpu.CompilerParams(
            collective_id=0, has_side_effects=True, vmem_limit_bytes=64000 * 1024
        ),
        name="render",
    )(
        slot_counts.reshape(N_TILE),
        brick_order.reshape(N_TILE),
        view_flip,
        tf_centers,
        tf_amps,
        owned_blocks.reshape(64, 32768),
    )
    return image.reshape(4, 16, LANES)


def solution(mesh):
    in_specs = (P("depth", "tile", None), P("depth", None), P("depth", None), P(), P(), P())
    out_specs = P(None, "depth", "tile")
    return jax.shard_map(body, mesh=mesh, in_specs=in_specs, out_specs=out_specs, check_vma=False)
```

```python
import functools

import jax
import jax.numpy as jnp
from jax import lax
from jax.experimental import pallas as pl
from jax.experimental.pallas import tpu as pltpu
from jax.sharding import PartitionSpec as P

MESH = pl.DeviceIdType.MESH
BLOCK = 32
KNOTS = 8
N_TILE = 16
N_DEPTH = 8
GROUPS = 4
LANES = 128
PIXELS = BLOCK * BLOCK
STEP = 1.5 / 512
HALF = 8
WIDE = 256
LOG2E = 1.4426950408889634
SPAN = 8
SPANS = BLOCK // SPAN
QUARTERS = PIXELS // WIDE


def split(x):
    high = x.astype(jnp.bfloat16)
    return high, x - high.astype(jnp.float32)


def set_mix(mix, centers, amps):
    row = lax.broadcasted_iota(jnp.int32, (HALF, KNOTS * HALF), 0)
    column = lax.broadcasted_iota(jnp.int32, (HALF, KNOTS * HALF), 1)
    same = column % HALF == row
    block = column // HALF
    center = jnp.zeros(row.shape, jnp.float32)
    for k in range(KNOTS):
        center = jnp.where(block == k, centers[k], center)
    fall = jnp.exp(center * center * -4.0)
    for c in range(4):
        value = jnp.zeros(row.shape, jnp.float32)
        for k in range(KNOTS):
            value = jnp.where(block == k, amps[c][k], value)
        value = jnp.where(same, value * fall * (LOG2E if c == 3 else 0.5), 0.0)
        high, rest = split(value)
        parts = [high.astype(jnp.float32)] * 2 + [rest]
        mix[c * HALF : (c + 1) * HALF, :] = jnp.concatenate(parts, axis=1).astype(jnp.bfloat16)


def set_fields(vox, mix, fields, slopes, index):
    index = jnp.minimum(index, QUARTERS * GROUPS * SPANS - 1)
    row = pl.multiple_of(index // SPANS % GROUPS * N_TILE, N_TILE)
    first = index % SPANS * (SPAN * PIXELS) + index // (SPANS * GROUPS) * WIDE
    for u in range(SPAN):
        lane = pl.multiple_of(first + u * PIXELS, WIDE)
        both = vox[pl.ds(row, N_TILE), pl.ds(lane, WIDE)].astype(jnp.float32)
        for h in range(2):
            value = both[h * HALF : (h + 1) * HALF]
            slope = value * (4.0 * LOG2E)
            bump = jnp.concatenate([jnp.exp2(value * (s - slope)) for s in slopes], axis=0)
            high, rest = split(bump)
            parts = jnp.concatenate([high, rest.astype(jnp.bfloat16), high], axis=0)
            fields[u, h] = jnp.dot(mix[...], parts, preferred_element_type=jnp.float32)


def advance(fields, step_sign, carry):
    for u in range(SPAN):
        total, held, red, green, blue = carry
        field = [
            jnp.concatenate([fields[u, h, c * HALF : (c + 1) * HALF] for h in range(2)], axis=0)
            for c in range(4)
        ]
        total = total + jnp.log(1.0 + jnp.exp2(field[3]))
        now = jnp.exp2(total * step_sign)
        weight = held - now
        red = red + weight * jnp.tanh(field[0])
        green = green + weight * jnp.tanh(field[1])
        blue = blue + weight * jnp.tanh(field[2])
        carry = total, now, red, green, blue
    return carry


def march(vox, img, mix, even, odd, slopes, sign, quarter, group):
    step_sign = sign * (STEP * LOG2E)
    base = (quarter * GROUPS + group) * SPANS

    def body(i, carry):
        set_fields(vox, mix, odd, slopes, base + 2 * i + 1)
        carry = advance(even, step_sign, carry)
        set_fields(vox, mix, even, slopes, base + 2 * i + 2)
        return advance(odd, step_sign, carry)

    zero = jnp.zeros((N_TILE, WIDE), jnp.float32)
    total, held, red, green, blue = lax.fori_loop(
        0, SPANS // 2, body, (zero, zero + 1.0, zero, zero, zero)
    )
    through = jnp.exp2(total * (-STEP * LOG2E))
    scale = jnp.where(sign < 0.0, 0.5, -0.5 * through)
    values = [scale * ((1.0 - held) + colour) for colour in (red, green, blue)]
    values.append(1.0 - through)
    for c in range(4):
        for side in range(2):
            row = (side * 4 + c) * N_TILE
            img[row : row + N_TILE, :] = values[c][:, side * LANES : (side + 1) * LANES]


def over(nearer, farther):
    clear = 1.0 - nearer
    left = jnp.broadcast_to(clear[3:4], (4, LANES))
    right = jnp.broadcast_to(clear[7:8], (4, LANES))
    return nearer + jnp.concatenate([left, right], axis=0) * farther


def render(
    counts, order, flips, centers_ref, amps_ref, blocks, out,
    vox, img, mix, even, odd, send, recv0, recv1, recv2, recv3, dsend, drecv, starts, rows, found,
    load_sem, send_sem, recv_sem, dsend_sem, drecv_sem,
):
    me = lax.axis_index("tile")
    my_depth = lax.axis_index("depth")
    recv = (recv0, recv1, recv2, recv3)

    def load(m):
        part = pl.ds(pl.multiple_of(m * N_TILE, N_TILE), N_TILE)
        return pltpu.make_async_copy(blocks.at[part, :], vox.at[part, :], load_sem.at[m])

    for m in range(GROUPS):
        load(m).start()
    barrier = pltpu.get_barrier_semaphore()
    for o in range(1, N_TILE):
        pl.semaphore_signal(
            barrier, inc=1, device_id={"tile": (me + o) % N_TILE}, device_id_type=MESH
        )
    for o in range(1, N_DEPTH):
        pl.semaphore_signal(
            barrier, inc=1, device_id={"depth": (my_depth + o) % N_DEPTH}, device_id_type=MESH
        )

    running = jnp.int32(0)
    my_start = jnp.int32(0)
    my_position = jnp.int32(0)
    for i in range(N_TILE):
        starts[i] = running
        my_start = jnp.where(me == i, running, my_start)
        my_position = jnp.where(order[i] == me, i, my_position)
        running = running + counts[i]
    for o in range(N_TILE):
        tile = (me + o) % N_TILE
        position = jnp.int32(0)
        for i in range(N_TILE):
            position = jnp.where(order[i] == tile, i, position)
        rows[o] = (position - my_start) & (N_TILE - 1)

    def find(block, carry):
        for u in range(8):
            index = block * 8 + u
            wanted = index * N_TILE + my_position
            owner = jnp.int32(0)
            for hop in (8, 4, 2, 1):
                owner = jnp.where(starts[owner + hop] <= wanted, owner + hop, owner)
            depth = ((wanted - starts[owner]) >> 4) & (GROUPS - 1)
            found[index] = owner * GROUPS + depth
        return carry

    lax.fori_loop(0, N_TILE // 4, find, 0)
    my_flip = flips[me]
    slot = lax.broadcasted_iota(jnp.int32, (N_TILE, WIDE), 0)
    sign = jnp.full((N_TILE, WIDE), -1.0, jnp.float32)
    for s in range(N_TILE):
        flip = flips[order[(my_start + s) & (N_TILE - 1)]].astype(jnp.float32)
        sign = jnp.where(slot == s, 2.0 * flip - 1.0, sign)
    centers = [centers_ref[k] for k in range(KNOTS)]
    amps = [[amps_ref[c, k] for k in range(KNOTS)] for c in range(4)]
    set_mix(mix, centers, amps)
    slopes = [center * (8.0 * LOG2E) for center in centers]

    def exchange(q, o):
        return pltpu.make_async_remote_copy(
            src_ref=send.at[q, o],
            dst_ref=recv[q].at[pl.ds(me * GROUPS, GROUPS)],
            send_sem=send_sem.at[q, o],
            recv_sem=recv_sem.at[q, o],
            device_id={"tile": (me + o) % N_TILE},
            device_id_type=MESH,
        )

    def piece(m, o):
        return pltpu.make_async_remote_copy(
            src_ref=send.at[QUARTERS - 1, o, m],
            dst_ref=recv[QUARTERS - 1].at[me * GROUPS + m],
            send_sem=send_sem.at[QUARTERS - 1 + m, o],
            recv_sem=recv_sem.at[QUARTERS - 1 + m, o],
            device_id={"tile": (me + o) % N_TILE},
            device_id_type=MESH,
        )

    def share(q, by):
        return pltpu.make_async_remote_copy(
            src_ref=dsend.at[q, by],
            dst_ref=drecv.at[q % 2, my_depth],
            send_sem=dsend_sem.at[q, by],
            recv_sem=drecv_sem.at[q % 2, my_depth],
            device_id={"depth": 2 * by + q // 2},
            device_id_type=MESH,
        )

    def layers(q, by):
        parts = []
        for bx in range(4):
            low = found[by * 4 + bx]
            high = found[16 + by * 4 + bx]
            near = recv[q][jnp.where(my_flip == 1, high, low)]
            far = recv[q][jnp.where(my_flip == 1, low, high)]
            parts.append(over(near, far))
        return jnp.stack(parts, axis=0)

    def share_out(q):
        for j in range(1, 4):
            by = (my_depth // 2 + j) % 4
            dsend[q, by] = layers(q, by)
            share(q, by).start()
        by = my_depth // 2
        mine = layers(q, by)

        @pl.when(my_depth % 2 == q // 2)
        def _():
            drecv[q % 2, my_depth] = mine

        @pl.when(my_depth % 2 != q // 2)
        def _():
            dsend[q, by] = mine
            share(q, by).start()

    load(0).wait()
    set_fields(vox, mix, even, slopes, 0)
    for q in range(QUARTERS):

        def group(m, carry):
            if q == 0:

                @pl.when(m + 1 < GROUPS)
                def _():
                    load(m + 1).wait()

            march(vox, img, mix, even, odd, slopes, sign, q, m)
            for o in range(N_TILE):
                image = img[pl.ds(rows[o], 8, stride=N_TILE), :]
                if o == 0:
                    recv[q][me * GROUPS + m] = image
                else:
                    send[q, o, m] = image
            if q == QUARTERS - 1:
                for o in range(1, N_TILE):
                    piece(m, o).start()
            return carry

        lax.fori_loop(0, GROUPS, group, 0)
        if q == 0:
            pl.semaphore_wait(barrier, N_TILE + N_DEPTH - 2)
        if q < QUARTERS - 1:
            for o in range(1, N_TILE):
                exchange(q, o).start()
        if q > 0:
            for o in range(1, N_TILE):
                exchange(q - 1, o).wait_recv()
            share_out(q - 1)
    for m in range(GROUPS):
        for o in range(1, N_TILE):
            piece(m, o).wait_recv()
    share_out(QUARTERS - 1)

    def arrived(side, o):
        source = (my_depth + o) % N_DEPTH
        return pltpu.make_async_remote_copy(
            src_ref=dsend.at[side, 0],
            dst_ref=drecv.at[side, source],
            send_sem=dsend_sem.at[side, 0],
            recv_sem=drecv_sem.at[side, source],
            device_id={"depth": source},
            device_id_type=MESH,
        )

    for side in range(2):
        for o in range(1, N_DEPTH):
            arrived(side, o).wait_recv()
    lane_block = lax.broadcasted_iota(jnp.int32, (8, LANES), 1) // BLOCK
    for side in range(2):
        blended = [jnp.zeros((8, LANES), jnp.float32) for bx in range(4)]
        for i in range(N_DEPTH):
            level = jnp.where(my_flip == 1, i, N_DEPTH - 1 - i)
            layer = drecv[side, level]
            blended = [over(layer[bx], blended[bx]) for bx in range(4)]
        for y in range(4):
            line = blended[0]
            for bx in range(4):
                shift = (bx - y) * BLOCK % LANES
                moved = pltpu.roll(blended[bx], shift, 1) if shift else blended[bx]
                line = moved if bx == 0 else jnp.where(lane_block == bx, moved, line)
            for half in range(2):
                row = side * 8 + half * 4 + y
                out[pl.ds(row, 4, stride=16), :] = line[half * 4 : half * 4 + 4]

    for o in range(1, N_TILE):
        for q in range(QUARTERS - 1):
            exchange(q, o).wait_send()
        for m in range(GROUPS):
            piece(m, o).wait_send()
    for q in range(QUARTERS):
        for j in range(1, 4):
            share(q, (my_depth // 2 + j) % 4).wait_send()

        @pl.when(my_depth % 2 != q // 2)
        def _():
            share(q, my_depth // 2).wait_send()


def body(owned_blocks, slot_counts, brick_order, view_flip, tf_centers, tf_amps):
    smem = pl.BlockSpec(memory_space=pltpu.SMEM)
    image = pl.pallas_call(
        render,
        out_shape=jax.ShapeDtypeStruct((64, LANES), jnp.float32),
        in_specs=[smem] * 5 + [pl.BlockSpec(memory_space=pltpu.HBM)],
        out_specs=pl.BlockSpec(memory_space=pltpu.VMEM),
        scratch_shapes=[
            pltpu.VMEM((64, 32768), jnp.bfloat16),
            pltpu.VMEM((8 * N_TILE, LANES), jnp.float32),
            pltpu.VMEM((4 * HALF, 3 * KNOTS * HALF), jnp.bfloat16),
            pltpu.VMEM((SPAN, 2, 4 * HALF, WIDE), jnp.float32),
            pltpu.VMEM((SPAN, 2, 4 * HALF, WIDE), jnp.float32),
            pltpu.VMEM((QUARTERS, N_TILE, GROUPS, 8, LANES), jnp.float32),
            pltpu.VMEM((N_TILE * GROUPS, 8, LANES), jnp.float32),
            pltpu.VMEM((N_TILE * GROUPS, 8, LANES), jnp.float32),
            pltpu.VMEM((N_TILE * GROUPS, 8, LANES), jnp.float32),
            pltpu.VMEM((N_TILE * GROUPS, 8, LANES), jnp.float32),
            pltpu.VMEM((QUARTERS, 4, 4, 8, LANES), jnp.float32),
            pltpu.VMEM((2, N_DEPTH, 4, 8, LANES), jnp.float32),
            pltpu.SMEM((N_TILE,), jnp.int32),
            pltpu.SMEM((N_TILE,), jnp.int32),
            pltpu.SMEM((2 * N_TILE,), jnp.int32),
            pltpu.SemaphoreType.DMA((GROUPS,)),
            pltpu.SemaphoreType.DMA((QUARTERS - 1 + GROUPS, N_TILE)),
            pltpu.SemaphoreType.DMA((QUARTERS - 1 + GROUPS, N_TILE)),
            pltpu.SemaphoreType.DMA((QUARTERS, 4)),
            pltpu.SemaphoreType.DMA((2, N_DEPTH)),
        ],
        compiler_params=pltpu.CompilerParams(
            collective_id=0, has_side_effects=True, vmem_limit_bytes=64000 * 1024
        ),
        name="render",
    )(
        slot_counts.reshape(N_TILE),
        brick_order.reshape(N_TILE),
        view_flip,
        tf_centers,
        tf_amps,
        owned_blocks.reshape(64, 32768),
    )
    return image.reshape(4, 16, LANES)


def solution(mesh):
    in_specs = (P("depth", "tile", None), P("depth", None), P("depth", None), P(), P(), P())
    out_specs = P(None, "depth", "tile")
    return jax.shard_map(body, mesh=mesh, in_specs=in_specs, out_specs=out_specs, check_vma=False)
```

```python
import functools

import jax
import jax.numpy as jnp
from jax import lax
from jax.experimental import pallas as pl
from jax.experimental.pallas import tpu as pltpu
from jax.sharding import PartitionSpec as P

MESH = pl.DeviceIdType.MESH
BLOCK = 32
KNOTS = 8
N_TILE = 16
N_DEPTH = 8
GROUPS = 4
LANES = 128
PIXELS = BLOCK * BLOCK
STEP = 1.5 / 512
HALF = 8
WIDE = 256
LOG2E = 1.4426950408889634
SPAN = 16
SPANS = BLOCK // SPAN
QUARTERS = PIXELS // WIDE


def split(x):
    high = x.astype(jnp.bfloat16)
    return high, x - high.astype(jnp.float32)


def set_mix(mix, centers, amps):
    row = lax.broadcasted_iota(jnp.int32, (HALF, KNOTS * HALF), 0)
    column = lax.broadcasted_iota(jnp.int32, (HALF, KNOTS * HALF), 1)
    same = column % HALF == row
    block = column // HALF
    center = jnp.zeros(row.shape, jnp.float32)
    for k in range(KNOTS):
        center = jnp.where(block == k, centers[k], center)
    fall = jnp.exp(center * center * -4.0)
    for c in range(4):
        value = jnp.zeros(row.shape, jnp.float32)
        for k in range(KNOTS):
            value = jnp.where(block == k, amps[c][k], value)
        value = jnp.where(same, value * fall * (LOG2E if c == 3 else 0.5), 0.0)
        high, rest = split(value)
        parts = [high.astype(jnp.float32)] * 2 + [rest]
        mix[c * HALF : (c + 1) * HALF, :] = jnp.concatenate(parts, axis=1).astype(jnp.bfloat16)


def set_fields(vox, mix, fields, slopes, index):
    index = jnp.minimum(index, QUARTERS * GROUPS * SPANS - 1)
    row = pl.multiple_of(index // SPANS % GROUPS * N_TILE, N_TILE)
    first = index % SPANS * (SPAN * PIXELS) + index // (SPANS * GROUPS) * WIDE
    for u in range(SPAN):
        lane = pl.multiple_of(first + u * PIXELS, WIDE)
        both = vox[pl.ds(row, N_TILE), pl.ds(lane, WIDE)].astype(jnp.float32)
        for h in range(2):
            value = both[h * HALF : (h + 1) * HALF]
            slope = value * (4.0 * LOG2E)
            bump = jnp.concatenate([jnp.exp2(value * (s - slope)) for s in slopes], axis=0)
            high, rest = split(bump)
            parts = jnp.concatenate([high, rest.astype(jnp.bfloat16), high], axis=0)
            fields[u, h] = jnp.dot(mix[...], parts, preferred_element_type=jnp.float32)


def advance(fields, step_sign, carry):
    for u in range(SPAN):
        total, held, red, green, blue = carry
        field = [
            jnp.concatenate([fields[u, h, c * HALF : (c + 1) * HALF] for h in range(2)], axis=0)
            for c in range(4)
        ]
        total = total + lax.log2(1.0 + jnp.exp2(field[3]))
        now = jnp.exp2(total * step_sign)
        weight = held - now
        red = red + weight * jnp.tanh(field[0])
        green = green + weight * jnp.tanh(field[1])
        blue = blue + weight * jnp.tanh(field[2])
        carry = total, now, red, green, blue
    return carry


def march(vox, img, mix, even, odd, slopes, sign, quarter, group):
    step_sign = sign * STEP
    base = (quarter * GROUPS + group) * SPANS

    def body(i, carry):
        set_fields(vox, mix, odd, slopes, base + 2 * i + 1)
        carry = advance(even, step_sign, carry)
        set_fields(vox, mix, even, slopes, base + 2 * i + 2)
        return advance(odd, step_sign, carry)

    zero = jnp.zeros((N_TILE, WIDE), jnp.float32)
    total, held, red, green, blue = lax.fori_loop(
        0, SPANS // 2, body, (zero, zero + 1.0, zero, zero, zero)
    )
    through = jnp.exp2(total * -STEP)
    scale = jnp.where(sign < 0.0, 0.5, -0.5 * through)
    values = [scale * ((1.0 - held) + colour) for colour in (red, green, blue)]
    values.append(1.0 - through)
    for c in range(4):
        for side in range(2):
            row = (side * 4 + c) * N_TILE
            img[row : row + N_TILE, :] = values[c][:, side * LANES : (side + 1) * LANES]


def over(nearer, farther):
    clear = 1.0 - nearer
    left = jnp.broadcast_to(clear[3:4], (4, LANES))
    right = jnp.broadcast_to(clear[7:8], (4, LANES))
    return nearer + jnp.concatenate([left, right], axis=0) * farther


def render(
    counts, order, flips, centers_ref, amps_ref, blocks, out,
    vox, img, mix, even, odd, send, recv0, recv1, recv2, recv3, dsend, drecv, starts, rows, found,
    load_sem, send_sem, recv_sem, dsend_sem, drecv_sem,
):
    me = lax.axis_index("tile")
    my_depth = lax.axis_index("depth")
    recv = (recv0, recv1, recv2, recv3)

    def load(m):
        part = pl.ds(pl.multiple_of(m * N_TILE, N_TILE), N_TILE)
        return pltpu.make_async_copy(blocks.at[part, :], vox.at[part, :], load_sem.at[m])

    for m in range(GROUPS):
        load(m).start()
    barrier = pltpu.get_barrier_semaphore()
    for o in range(1, N_TILE):
        pl.semaphore_signal(
            barrier, inc=1, device_id={"tile": (me + o) % N_TILE}, device_id_type=MESH
        )
    for o in range(1, N_DEPTH):
        pl.semaphore_signal(
            barrier, inc=1, device_id={"depth": (my_depth + o) % N_DEPTH}, device_id_type=MESH
        )

    running = jnp.int32(0)
    my_start = jnp.int32(0)
    my_position = jnp.int32(0)
    for i in range(N_TILE):
        starts[i] = running
        my_start = jnp.where(me == i, running, my_start)
        my_position = jnp.where(order[i] == me, i, my_position)
        running = running + counts[i]
    for o in range(N_TILE):
        tile = (me + o) % N_TILE
        position = jnp.int32(0)
        for i in range(N_TILE):
            position = jnp.where(order[i] == tile, i, position)
        rows[o] = (position - my_start) & (N_TILE - 1)

    def find(block, carry):
        for u in range(8):
            index = block * 8 + u
            wanted = index * N_TILE + my_position
            owner = jnp.int32(0)
            for hop in (8, 4, 2, 1):
                owner = jnp.where(starts[owner + hop] <= wanted, owner + hop, owner)
            depth = ((wanted - starts[owner]) >> 4) & (GROUPS - 1)
            found[index] = owner * GROUPS + depth
        return carry

    lax.fori_loop(0, N_TILE // 4, find, 0)
    my_flip = flips[me]
    slot = lax.broadcasted_iota(jnp.int32, (N_TILE, WIDE), 0)
    sign = jnp.full((N_TILE, WIDE), -1.0, jnp.float32)
    for s in range(N_TILE):
        flip = flips[order[(my_start + s) & (N_TILE - 1)]].astype(jnp.float32)
        sign = jnp.where(slot == s, 2.0 * flip - 1.0, sign)
    centers = [centers_ref[k] for k in range(KNOTS)]
    amps = [[amps_ref[c, k] for k in range(KNOTS)] for c in range(4)]
    set_mix(mix, centers, amps)
    slopes = [center * (8.0 * LOG2E) for center in centers]

    def exchange(q, o):
        return pltpu.make_async_remote_copy(
            src_ref=send.at[q, o],
            dst_ref=recv[q].at[pl.ds(me * GROUPS, GROUPS)],
            send_sem=send_sem.at[q, o],
            recv_sem=recv_sem.at[q, o],
            device_id={"tile": (me + o) % N_TILE},
            device_id_type=MESH,
        )

    def piece(m, o):
        return pltpu.make_async_remote_copy(
            src_ref=send.at[QUARTERS - 1, o, m],
            dst_ref=recv[QUARTERS - 1].at[me * GROUPS + m],
            send_sem=send_sem.at[QUARTERS - 1 + m, o],
            recv_sem=recv_sem.at[QUARTERS - 1 + m, o],
            device_id={"tile": (me + o) % N_TILE},
            device_id_type=MESH,
        )

    def share(q, by):
        return pltpu.make_async_remote_copy(
            src_ref=dsend.at[q, by],
            dst_ref=drecv.at[q % 2, my_depth],
            send_sem=dsend_sem.at[q, by],
            recv_sem=drecv_sem.at[q % 2, my_depth],
            device_id={"depth": 2 * by + q // 2},
            device_id_type=MESH,
        )

    def layers(q, by):
        parts = []
        for bx in range(4):
            low = found[by * 4 + bx]
            high = found[16 + by * 4 + bx]
            near = recv[q][jnp.where(my_flip == 1, high, low)]
            far = recv[q][jnp.where(my_flip == 1, low, high)]
            parts.append(over(near, far))
        return jnp.stack(parts, axis=0)

    def share_out(q):
        for j in range(1, 4):
            by = (my_depth // 2 + j) % 4
            dsend[q, by] = layers(q, by)
            share(q, by).start()
        by = my_depth // 2
        mine = layers(q, by)

        @pl.when(my_depth % 2 == q // 2)
        def _():
            drecv[q % 2, my_depth] = mine

        @pl.when(my_depth % 2 != q // 2)
        def _():
            dsend[q, by] = mine
            share(q, by).start()

    def shared(q):
        for j in range(1, 4):
            share(q, (my_depth // 2 + j) % 4).wait_send()

        @pl.when(my_depth % 2 != q // 2)
        def _():
            share(q, my_depth // 2).wait_send()

    load(0).wait()
    set_fields(vox, mix, even, slopes, 0)
    for q in range(QUARTERS):

        def group(m, carry):
            if q == 0:

                @pl.when(m + 1 < GROUPS)
                def _():
                    load(m + 1).wait()

            march(vox, img, mix, even, odd, slopes, sign, q, m)
            for o in range(N_TILE):
                image = img[pl.ds(rows[o], 8, stride=N_TILE), :]
                if o == 0:
                    recv[q][me * GROUPS + m] = image
                else:
                    send[q, o, m] = image
            if q == QUARTERS - 1:
                for o in range(1, N_TILE):
                    piece(m, o).start()
            return carry

        lax.fori_loop(0, GROUPS, group, 0)
        if q == 0:
            pl.semaphore_wait(barrier, N_TILE + N_DEPTH - 2)
        if q < QUARTERS - 1:
            for o in range(1, N_TILE):
                exchange(q, o).start()
        if q > 0:
            for o in range(1, N_TILE):
                exchange(q - 1, o).wait_recv()
            share_out(q - 1)
    for o in range(1, N_TILE):
        for q in range(QUARTERS - 1):
            exchange(q, o).wait_send()
    for q in range(QUARTERS - 1):
        shared(q)
    for m in range(GROUPS):
        for o in range(1, N_TILE):
            piece(m, o).wait_recv()
    share_out(QUARTERS - 1)
    for m in range(GROUPS):
        for o in range(1, N_TILE):
            piece(m, o).wait_send()

    def arrived(side, o):
        source = (my_depth + o) % N_DEPTH
        return pltpu.make_async_remote_copy(
            src_ref=dsend.at[side, 0],
            dst_ref=drecv.at[side, source],
            send_sem=dsend_sem.at[side, 0],
            recv_sem=drecv_sem.at[side, source],
            device_id={"depth": source},
            device_id_type=MESH,
        )

    for side in range(2):
        for o in range(1, N_DEPTH):
            arrived(side, o).wait_recv()
    lane_block = lax.broadcasted_iota(jnp.int32, (8, LANES), 1) // BLOCK
    for side in range(2):
        blended = [jnp.zeros((8, LANES), jnp.float32) for bx in range(4)]
        for i in range(N_DEPTH):
            level = jnp.where(my_flip == 1, i, N_DEPTH - 1 - i)
            layer = drecv[side, level]
            blended = [over(layer[bx], blended[bx]) for bx in range(4)]
        for y in range(4):
            line = blended[0]
            for bx in range(4):
                shift = (bx - y) * BLOCK % LANES
                moved = pltpu.roll(blended[bx], shift, 1) if shift else blended[bx]
                line = moved if bx == 0 else jnp.where(lane_block == bx, moved, line)
            for half in range(2):
                row = side * 8 + half * 4 + y
                out[pl.ds(row, 4, stride=16), :] = line[half * 4 : half * 4 + 4]
    shared(QUARTERS - 1)


def body(owned_blocks, slot_counts, brick_order, view_flip, tf_centers, tf_amps):
    smem = pl.BlockSpec(memory_space=pltpu.SMEM)
    image = pl.pallas_call(
        render,
        out_shape=jax.ShapeDtypeStruct((64, LANES), jnp.float32),
        in_specs=[smem] * 5 + [pl.BlockSpec(memory_space=pltpu.HBM)],
        out_specs=pl.BlockSpec(memory_space=pltpu.VMEM),
        scratch_shapes=[
            pltpu.VMEM((64, 32768), jnp.bfloat16),
            pltpu.VMEM((8 * N_TILE, LANES), jnp.float32),
            pltpu.VMEM((4 * HALF, 3 * KNOTS * HALF), jnp.bfloat16),
            pltpu.VMEM((SPAN, 2, 4 * HALF, WIDE), jnp.float32),
            pltpu.VMEM((SPAN, 2, 4 * HALF, WIDE), jnp.float32),
            pltpu.VMEM((QUARTERS, N_TILE, GROUPS, 8, LANES), jnp.float32),
            pltpu.VMEM((N_TILE * GROUPS, 8, LANES), jnp.float32),
            pltpu.VMEM((N_TILE * GROUPS, 8, LANES), jnp.float32),
            pltpu.VMEM((N_TILE * GROUPS, 8, LANES), jnp.float32),
            pltpu.VMEM((N_TILE * GROUPS, 8, LANES), jnp.float32),
            pltpu.VMEM((QUARTERS, 4, 4, 8, LANES), jnp.float32),
            pltpu.VMEM((2, N_DEPTH, 4, 8, LANES), jnp.float32),
            pltpu.SMEM((N_TILE,), jnp.int32),
            pltpu.SMEM((N_TILE,), jnp.int32),
            pltpu.SMEM((2 * N_TILE,), jnp.int32),
            pltpu.SemaphoreType.DMA((GROUPS,)),
            pltpu.SemaphoreType.DMA((QUARTERS - 1 + GROUPS, N_TILE)),
            pltpu.SemaphoreType.DMA((QUARTERS - 1 + GROUPS, N_TILE)),
            pltpu.SemaphoreType.DMA((QUARTERS, 4)),
            pltpu.SemaphoreType.DMA((2, N_DEPTH)),
        ],
        compiler_params=pltpu.CompilerParams(
            collective_id=0, has_side_effects=True, vmem_limit_bytes=64000 * 1024
        ),
        name="render",
    )(
        slot_counts.reshape(N_TILE),
        brick_order.reshape(N_TILE),
        view_flip,
        tf_centers,
        tf_amps,
        owned_blocks.reshape(64, 32768),
    )
    return image.reshape(4, 16, LANES)


def solution(mesh):
    in_specs = (P("depth", "tile", None), P("depth", None), P("depth", None), P(), P(), P())
    out_specs = P(None, "depth", "tile")
    return jax.shard_map(body, mesh=mesh, in_specs=in_specs, out_specs=out_specs, check_vma=False)
```

```python
import functools

import jax
import jax.numpy as jnp
from jax import lax
from jax.experimental import pallas as pl
from jax.experimental.pallas import tpu as pltpu
from jax.sharding import PartitionSpec as P

MESH = pl.DeviceIdType.MESH
BLOCK = 32
KNOTS = 8
N_TILE = 16
N_DEPTH = 8
GROUPS = 4
LANES = 128
PIXELS = BLOCK * BLOCK
STEP = 1.5 / 512
HALF = 8
WIDE = 256
LOG2E = 1.4426950408889634
SPAN = 16
JOIN = 4
SPANS = BLOCK // SPAN
QUARTERS = PIXELS // WIDE


def set_mix(mix, centers, amps):
    row = lax.broadcasted_iota(jnp.int32, (HALF, KNOTS * HALF), 0)
    column = lax.broadcasted_iota(jnp.int32, (HALF, KNOTS * HALF), 1)
    same = column % HALF == row
    block = column // HALF
    center = jnp.zeros(row.shape, jnp.float32)
    for k in range(KNOTS):
        center = jnp.where(block == k, centers[k], center)
    fall = jnp.exp(center * center * -4.0)
    for c in range(4):
        value = jnp.zeros(row.shape, jnp.float32)
        for k in range(KNOTS):
            value = jnp.where(block == k, amps[c][k], value)
        value = jnp.where(same, value * fall * (LOG2E if c == 3 else 0.5), 0.0)
        mix[c * HALF : (c + 1) * HALF, :] = value


def set_fields(vox, mix, fields, slopes, index):
    index = jnp.minimum(index, QUARTERS * GROUPS * SPANS - 1)
    row = pl.multiple_of(index // SPANS % GROUPS * N_TILE, N_TILE)
    first = index % SPANS * (SPAN * PIXELS) + index // (SPANS * GROUPS) * WIDE
    for start in range(0, SPAN, JOIN):
        halves = ([], [])
        for u in range(start, start + JOIN):
            lane = pl.multiple_of(first + u * PIXELS, WIDE)
            both = vox[pl.ds(row, N_TILE), pl.ds(lane, WIDE)].astype(jnp.float32)
            for h in range(2):
                value = both[h * HALF : (h + 1) * HALF]
                slope = value * (4.0 * LOG2E)
                bumps = [jnp.exp2(value * (s - slope)) for s in slopes]
                halves[h].append(jnp.concatenate(bumps, axis=0))
        for h in range(2):
            mixed = jnp.dot(
                mix[...],
                jnp.concatenate(halves[h], axis=1),
                preferred_element_type=jnp.float32,
                precision=lax.Precision.HIGH,
            )
            for u in range(JOIN):
                fields[start + u, h] = mixed[:, u * WIDE : (u + 1) * WIDE]


def advance(fields, step_sign, carry):
    for u in range(SPAN):
        total, held, red, green, blue = carry
        field = [
            jnp.concatenate([fields[u, h, c * HALF : (c + 1) * HALF] for h in range(2)], axis=0)
            for c in range(4)
        ]
        total = total + lax.log2(1.0 + jnp.exp2(field[3]))
        now = jnp.exp2(total * step_sign)
        weight = held - now
        red = red + weight * jnp.tanh(field[0])
        green = green + weight * jnp.tanh(field[1])
        blue = blue + weight * jnp.tanh(field[2])
        carry = total, now, red, green, blue
    return carry


def march(vox, img, mix, even, odd, slopes, sign, quarter, group):
    step_sign = sign * STEP
    base = (quarter * GROUPS + group) * SPANS

    def body(i, carry):
        set_fields(vox, mix, odd, slopes, base + 2 * i + 1)
        carry = advance(even, step_sign, carry)
        set_fields(vox, mix, even, slopes, base + 2 * i + 2)
        return advance(odd, step_sign, carry)

    zero = jnp.zeros((N_TILE, WIDE), jnp.float32)
    total, held, red, green, blue = lax.fori_loop(
        0, SPANS // 2, body, (zero, zero + 1.0, zero, zero, zero)
    )
    through = jnp.exp2(total * -STEP)
    scale = jnp.where(sign < 0.0, 0.5, -0.5 * through)
    values = [scale * ((1.0 - held) + colour) for colour in (red, green, blue)]
    values.append(1.0 - through)
    for c in range(4):
        for side in range(2):
            row = (side * 4 + c) * N_TILE
            img[row : row + N_TILE, :] = values[c][:, side * LANES : (side + 1) * LANES]


def over(nearer, farther):
    clear = 1.0 - nearer
    left = jnp.broadcast_to(clear[3:4], (4, LANES))
    right = jnp.broadcast_to(clear[7:8], (4, LANES))
    return nearer + jnp.concatenate([left, right], axis=0) * farther


def render(
    counts, order, flips, centers_ref, amps_ref, blocks, out,
    vox, img, mix, even, odd, send, recv0, recv1, recv2, recv3, dsend, drecv, starts, rows, found,
    load_sem, send_sem, recv_sem, dsend_sem, drecv_sem,
):
    me = lax.axis_index("tile")
    my_depth = lax.axis_index("depth")
    recv = (recv0, recv1, recv2, recv3)

    def load(m):
        part = pl.ds(pl.multiple_of(m * N_TILE, N_TILE), N_TILE)
        return pltpu.make_async_copy(blocks.at[part, :], vox.at[part, :], load_sem.at[m])

    for m in range(GROUPS):
        load(m).start()
    barrier = pltpu.get_barrier_semaphore()
    for o in range(1, N_TILE):
        pl.semaphore_signal(
            barrier, inc=1, device_id={"tile": (me + o) % N_TILE}, device_id_type=MESH
        )
    for o in range(1, N_DEPTH):
        pl.semaphore_signal(
            barrier, inc=1, device_id={"depth": (my_depth + o) % N_DEPTH}, device_id_type=MESH
        )

    running = jnp.int32(0)
    my_start = jnp.int32(0)
    my_position = jnp.int32(0)
    for i in range(N_TILE):
        starts[i] = running
        my_start = jnp.where(me == i, running, my_start)
        my_position = jnp.where(order[i] == me, i, my_position)
        running = running + counts[i]
    for o in range(N_TILE):
        tile = (me + o) % N_TILE
        position = jnp.int32(0)
        for i in range(N_TILE):
            position = jnp.where(order[i] == tile, i, position)
        rows[o] = (position - my_start) & (N_TILE - 1)

    def find(block, carry):
        for u in range(8):
            index = block * 8 + u
            wanted = index * N_TILE + my_position
            owner = jnp.int32(0)
            for hop in (8, 4, 2, 1):
                owner = jnp.where(starts[owner + hop] <= wanted, owner + hop, owner)
            depth = ((wanted - starts[owner]) >> 4) & (GROUPS - 1)
            found[index] = owner * GROUPS + depth
        return carry

    lax.fori_loop(0, N_TILE // 4, find, 0)
    my_flip = flips[me]
    slot = lax.broadcasted_iota(jnp.int32, (N_TILE, WIDE), 0)
    sign = jnp.full((N_TILE, WIDE), -1.0, jnp.float32)
    for s in range(N_TILE):
        flip = flips[order[(my_start + s) & (N_TILE - 1)]].astype(jnp.float32)
        sign = jnp.where(slot == s, 2.0 * flip - 1.0, sign)
    centers = [centers_ref[k] for k in range(KNOTS)]
    amps = [[amps_ref[c, k] for k in range(KNOTS)] for c in range(4)]
    set_mix(mix, centers, amps)
    slopes = [center * (8.0 * LOG2E) for center in centers]

    def exchange(q, o):
        return pltpu.make_async_remote_copy(
            src_ref=send.at[q, o],
            dst_ref=recv[q].at[pl.ds(me * GROUPS, GROUPS)],
            send_sem=send_sem.at[q, o],
            recv_sem=recv_sem.at[q, o],
            device_id={"tile": (me + o) % N_TILE},
            device_id_type=MESH,
        )

    def piece(m, o):
        return pltpu.make_async_remote_copy(
            src_ref=send.at[QUARTERS - 1, o, m],
            dst_ref=recv[QUARTERS - 1].at[me * GROUPS + m],
            send_sem=send_sem.at[QUARTERS - 1 + m, o],
            recv_sem=recv_sem.at[QUARTERS - 1 + m, o],
            device_id={"tile": (me + o) % N_TILE},
            device_id_type=MESH,
        )

    def share(q, by):
        return pltpu.make_async_remote_copy(
            src_ref=dsend.at[q, by],
            dst_ref=drecv.at[q % 2, my_depth],
            send_sem=dsend_sem.at[q, by],
            recv_sem=drecv_sem.at[q % 2, my_depth],
            device_id={"depth": 2 * by + q // 2},
            device_id_type=MESH,
        )

    def layers(q, by):
        parts = []
        for bx in range(4):
            low = found[by * 4 + bx]
            high = found[16 + by * 4 + bx]
            near = recv[q][jnp.where(my_flip == 1, high, low)]
            far = recv[q][jnp.where(my_flip == 1, low, high)]
            parts.append(over(near, far))
        return jnp.stack(parts, axis=0)

    def share_out(q):
        for j in range(1, 4):
            by = (my_depth // 2 + j) % 4
            dsend[q, by] = layers(q, by)
            share(q, by).start()
        by = my_depth // 2
        mine = layers(q, by)

        @pl.when(my_depth % 2 == q // 2)
        def _():
            drecv[q % 2, my_depth] = mine

        @pl.when(my_depth % 2 != q // 2)
        def _():
            dsend[q, by] = mine
            share(q, by).start()

    def shared(q):
        for j in range(1, 4):
            share(q, (my_depth // 2 + j) % 4).wait_send()

        @pl.when(my_depth % 2 != q // 2)
        def _():
            share(q, my_depth // 2).wait_send()

    load(0).wait()
    set_fields(vox, mix, even, slopes, 0)
    for q in range(QUARTERS):

        def group(m, carry):
            if q == 0:

                @pl.when(m + 1 < GROUPS)
                def _():
                    load(m + 1).wait()

            march(vox, img, mix, even, odd, slopes, sign, q, m)
            for o in range(N_TILE):
                image = img[pl.ds(rows[o], 8, stride=N_TILE), :]
                if o == 0:
                    recv[q][me * GROUPS + m] = image
                else:
                    send[q, o, m] = image
            if q == QUARTERS - 1:
                for o in range(1, N_TILE):
                    piece(m, o).start()
            return carry

        lax.fori_loop(0, GROUPS, group, 0)
        if q == 0:
            pl.semaphore_wait(barrier, N_TILE + N_DEPTH - 2)
        if q < QUARTERS - 1:
            for o in range(1, N_TILE):
                exchange(q, o).start()
        if q > 0:
            for o in range(1, N_TILE):
                exchange(q - 1, o).wait_recv()
            share_out(q - 1)
    for o in range(1, N_TILE):
        for q in range(QUARTERS - 1):
            exchange(q, o).wait_send()
    for q in range(QUARTERS - 1):
        shared(q)
    for m in range(GROUPS):
        for o in range(1, N_TILE):
            piece(m, o).wait_recv()
    share_out(QUARTERS - 1)
    for m in range(GROUPS):
        for o in range(1, N_TILE):
            piece(m, o).wait_send()

    def arrived(side, o):
        source = (my_depth + o) % N_DEPTH
        return pltpu.make_async_remote_copy(
            src_ref=dsend.at[side, 0],
            dst_ref=drecv.at[side, source],
            send_sem=dsend_sem.at[side, 0],
            recv_sem=drecv_sem.at[side, source],
            device_id={"depth": source},
            device_id_type=MESH,
        )

    for side in range(2):
        for o in range(1, N_DEPTH):
            arrived(side, o).wait_recv()
    lane_block = lax.broadcasted_iota(jnp.int32, (8, LANES), 1) // BLOCK
    for side in range(2):
        blended = [jnp.zeros((8, LANES), jnp.float32) for bx in range(4)]
        for i in range(N_DEPTH):
            level = jnp.where(my_flip == 1, i, N_DEPTH - 1 - i)
            layer = drecv[side, level]
            blended = [over(layer[bx], blended[bx]) for bx in range(4)]
        for y in range(4):
            line = blended[0]
            for bx in range(4):
                shift = (bx - y) * BLOCK % LANES
                moved = pltpu.roll(blended[bx], shift, 1) if shift else blended[bx]
                line = moved if bx == 0 else jnp.where(lane_block == bx, moved, line)
            for half in range(2):
                row = side * 8 + half * 4 + y
                out[pl.ds(row, 4, stride=16), :] = line[half * 4 : half * 4 + 4]
    shared(QUARTERS - 1)


def body(owned_blocks, slot_counts, brick_order, view_flip, tf_centers, tf_amps):
    smem = pl.BlockSpec(memory_space=pltpu.SMEM)
    image = pl.pallas_call(
        render,
        out_shape=jax.ShapeDtypeStruct((64, LANES), jnp.float32),
        in_specs=[smem] * 5 + [pl.BlockSpec(memory_space=pltpu.HBM)],
        out_specs=pl.BlockSpec(memory_space=pltpu.VMEM),
        scratch_shapes=[
            pltpu.VMEM((64, 32768), jnp.bfloat16),
            pltpu.VMEM((8 * N_TILE, LANES), jnp.float32),
            pltpu.VMEM((4 * HALF, KNOTS * HALF), jnp.float32),
            pltpu.VMEM((SPAN, 2, 4 * HALF, WIDE), jnp.float32),
            pltpu.VMEM((SPAN, 2, 4 * HALF, WIDE), jnp.float32),
            pltpu.VMEM((QUARTERS, N_TILE, GROUPS, 8, LANES), jnp.float32),
            pltpu.VMEM((N_TILE * GROUPS, 8, LANES), jnp.float32),
            pltpu.VMEM((N_TILE * GROUPS, 8, LANES), jnp.float32),
            pltpu.VMEM((N_TILE * GROUPS, 8, LANES), jnp.float32),
            pltpu.VMEM((N_TILE * GROUPS, 8, LANES), jnp.float32),
            pltpu.VMEM((QUARTERS, 4, 4, 8, LANES), jnp.float32),
            pltpu.VMEM((2, N_DEPTH, 4, 8, LANES), jnp.float32),
            pltpu.SMEM((N_TILE,), jnp.int32),
            pltpu.SMEM((N_TILE,), jnp.int32),
            pltpu.SMEM((2 * N_TILE,), jnp.int32),
            pltpu.SemaphoreType.DMA((GROUPS,)),
            pltpu.SemaphoreType.DMA((QUARTERS - 1 + GROUPS, N_TILE)),
            pltpu.SemaphoreType.DMA((QUARTERS - 1 + GROUPS, N_TILE)),
            pltpu.SemaphoreType.DMA((QUARTERS, 4)),
            pltpu.SemaphoreType.DMA((2, N_DEPTH)),
        ],
        compiler_params=pltpu.CompilerParams(
            collective_id=0, has_side_effects=True, vmem_limit_bytes=64000 * 1024
        ),
        name="render",
    )(
        slot_counts.reshape(N_TILE),
        brick_order.reshape(N_TILE),
        view_flip,
        tf_centers,
        tf_amps,
        owned_blocks.reshape(64, 32768),
    )
    return image.reshape(4, 16, LANES)


def solution(mesh):
    in_specs = (P("depth", "tile", None), P("depth", None), P("depth", None), P(), P(), P())
    out_specs = P(None, "depth", "tile")
    return jax.shard_map(body, mesh=mesh, in_specs=in_specs, out_specs=out_specs, check_vma=False)
```

```python
import functools

import jax
import jax.numpy as jnp
from jax import lax
from jax.experimental import pallas as pl
from jax.experimental.pallas import tpu as pltpu
from jax.sharding import PartitionSpec as P

MESH = pl.DeviceIdType.MESH
BLOCK = 32
KNOTS = 8
N_TILE = 16
N_DEPTH = 8
GROUPS = 4
LANES = 128
PIXELS = BLOCK * BLOCK
STEP = 1.5 / 512
HALF = 8
WIDE = 256
LOG2E = 1.4426950408889634
SPAN = 16
JOIN = 4
SPANS = BLOCK // SPAN
QUARTERS = PIXELS // WIDE


def set_mix(mix, centers, amps):
    row = lax.broadcasted_iota(jnp.int32, (HALF, KNOTS * HALF), 0)
    column = lax.broadcasted_iota(jnp.int32, (HALF, KNOTS * HALF), 1)
    same = column % HALF == row
    block = column // HALF
    center = jnp.zeros(row.shape, jnp.float32)
    for k in range(KNOTS):
        center = jnp.where(block == k, centers[k], center)
    fall = jnp.exp(center * center * -4.0)
    for c in range(4):
        value = jnp.zeros(row.shape, jnp.float32)
        for k in range(KNOTS):
            value = jnp.where(block == k, amps[c][k], value)
        value = jnp.where(same, value * fall * (LOG2E if c == 3 else 0.5), 0.0)
        mix[c * HALF : (c + 1) * HALF, :] = value


def set_fields(vox, mix, fields, slopes, index):
    index = jnp.minimum(index, QUARTERS * GROUPS * SPANS - 1)
    row = pl.multiple_of(index // SPANS % GROUPS * N_TILE, N_TILE)
    first = index % SPANS * (SPAN * PIXELS) + index // (SPANS * GROUPS) * WIDE
    for start in range(0, SPAN, JOIN):
        halves = ([], [])
        for u in range(start, start + JOIN):
            lane = pl.multiple_of(first + u * PIXELS, WIDE)
            both = vox[pl.ds(row, N_TILE), pl.ds(lane, WIDE)].astype(jnp.float32)
            for h in range(2):
                value = both[h * HALF : (h + 1) * HALF]
                slope = value * (4.0 * LOG2E)
                bumps = [jnp.exp2(value * (s - slope)) for s in slopes]
                halves[h].append(jnp.concatenate(bumps, axis=0))
        for h in range(2):
            mixed = jnp.dot(
                mix[...],
                jnp.concatenate(halves[h], axis=1),
                preferred_element_type=jnp.float32,
                precision=lax.Precision.HIGH,
            )
            for u in range(JOIN):
                fields[start + u, h] = mixed[:, u * WIDE : (u + 1) * WIDE]


def advance(fields, step_sign, carry):
    for u in range(SPAN):
        total, held, red, green, blue = carry
        field = [
            jnp.concatenate([fields[u, h, c * HALF : (c + 1) * HALF] for h in range(2)], axis=0)
            for c in range(4)
        ]
        total = total + lax.log2(1.0 + jnp.exp2(field[3]))
        now = jnp.exp2(total * step_sign)
        weight = held - now
        red = red + weight * jnp.tanh(field[0])
        green = green + weight * jnp.tanh(field[1])
        blue = blue + weight * jnp.tanh(field[2])
        carry = total, now, red, green, blue
    return carry


def march(vox, img, mix, even, odd, slopes, sign, quarter, group, last):
    step_sign = sign * STEP
    base = (quarter * GROUPS + group) * SPANS

    def body(i, carry):
        set_fields(vox, mix, odd, slopes, base + 2 * i + 1)
        carry = advance(even, step_sign, carry)
        if not last:
            set_fields(vox, mix, even, slopes, base + 2 * i + 2)
        return advance(odd, step_sign, carry)

    zero = jnp.zeros((N_TILE, WIDE), jnp.float32)
    total, held, red, green, blue = lax.fori_loop(
        0, SPANS // 2, body, (zero, zero + 1.0, zero, zero, zero)
    )
    through = jnp.exp2(total * -STEP)
    scale = jnp.where(sign < 0.0, 0.5, -0.5 * through)
    values = [scale * ((1.0 - held) + colour) for colour in (red, green, blue)]
    values.append(1.0 - through)
    for c in range(4):
        for side in range(2):
            row = (side * 4 + c) * N_TILE
            img[row : row + N_TILE, :] = values[c][:, side * LANES : (side + 1) * LANES]


def over(nearer, farther):
    clear = 1.0 - nearer
    left = jnp.broadcast_to(clear[3:4], (4, LANES))
    right = jnp.broadcast_to(clear[7:8], (4, LANES))
    return nearer + jnp.concatenate([left, right], axis=0) * farther


def render(
    counts, order, flips, centers_ref, amps_ref, blocks, out,
    vox, img, mix, even, odd, send, recv0, recv1, recv2, recv3, dsend, drecv, starts, rows, found,
    load_sem, send_sem, recv_sem, dsend_sem, drecv_sem,
):
    me = lax.axis_index("tile")
    my_depth = lax.axis_index("depth")
    recv = (recv0, recv1, recv2, recv3)

    def load(m):
        part = pl.ds(pl.multiple_of(m * N_TILE, N_TILE), N_TILE)
        return pltpu.make_async_copy(blocks.at[part, :], vox.at[part, :], load_sem.at[m])

    def first(part):
        cells = pl.ds(part * SPAN * PIXELS, SPAN * PIXELS)
        rows_in = pl.ds(0, N_TILE)
        return pltpu.make_async_copy(
            blocks.at[rows_in, cells], vox.at[rows_in, cells], load_sem.at[part * GROUPS]
        )

    for part in range(2):
        first(part).start()
    for m in range(1, GROUPS):
        load(m).start()
    barrier = pltpu.get_barrier_semaphore()
    for o in range(1, N_TILE):
        pl.semaphore_signal(
            barrier, inc=1, device_id={"tile": (me + o) % N_TILE}, device_id_type=MESH
        )
    for o in range(1, N_DEPTH):
        pl.semaphore_signal(
            barrier, inc=1, device_id={"depth": (my_depth + o) % N_DEPTH}, device_id_type=MESH
        )

    running = jnp.int32(0)
    my_start = jnp.int32(0)
    my_position = jnp.int32(0)
    for i in range(N_TILE):
        starts[i] = running
        my_start = jnp.where(me == i, running, my_start)
        my_position = jnp.where(order[i] == me, i, my_position)
        running = running + counts[i]
    for o in range(N_TILE):
        tile = (me + o) % N_TILE
        position = jnp.int32(0)
        for i in range(N_TILE):
            position = jnp.where(order[i] == tile, i, position)
        rows[o] = (position - my_start) & (N_TILE - 1)

    def find(block, carry):
        for u in range(8):
            index = block * 8 + u
            wanted = index * N_TILE + my_position
            owner = jnp.int32(0)
            for hop in (8, 4, 2, 1):
                owner = jnp.where(starts[owner + hop] <= wanted, owner + hop, owner)
            depth = ((wanted - starts[owner]) >> 4) & (GROUPS - 1)
            found[index] = owner * GROUPS + depth
        return carry

    lax.fori_loop(0, N_TILE // 4, find, 0)
    my_flip = flips[me]
    slot = lax.broadcasted_iota(jnp.int32, (N_TILE, WIDE), 0)
    sign = jnp.full((N_TILE, WIDE), -1.0, jnp.float32)
    for s in range(N_TILE):
        flip = flips[order[(my_start + s) & (N_TILE - 1)]].astype(jnp.float32)
        sign = jnp.where(slot == s, 2.0 * flip - 1.0, sign)
    centers = [centers_ref[k] for k in range(KNOTS)]
    amps = [[amps_ref[c, k] for k in range(KNOTS)] for c in range(4)]
    set_mix(mix, centers, amps)
    slopes = [center * (8.0 * LOG2E) for center in centers]

    def exchange(q, o):
        return pltpu.make_async_remote_copy(
            src_ref=send.at[q, o],
            dst_ref=recv[q].at[pl.ds(me * GROUPS, GROUPS)],
            send_sem=send_sem.at[q, o],
            recv_sem=recv_sem.at[q, o],
            device_id={"tile": (me + o) % N_TILE},
            device_id_type=MESH,
        )

    def piece(m, o):
        return pltpu.make_async_remote_copy(
            src_ref=send.at[QUARTERS - 1, o, m],
            dst_ref=recv[QUARTERS - 1].at[me * GROUPS + m],
            send_sem=send_sem.at[QUARTERS - 1 + m, o],
            recv_sem=recv_sem.at[QUARTERS - 1 + m, o],
            device_id={"tile": (me + o) % N_TILE},
            device_id_type=MESH,
        )

    def share(q, by):
        return pltpu.make_async_remote_copy(
            src_ref=dsend.at[q, by],
            dst_ref=drecv.at[q % 2, my_depth],
            send_sem=dsend_sem.at[q, by],
            recv_sem=drecv_sem.at[q % 2, my_depth],
            device_id={"depth": 2 * by + q // 2},
            device_id_type=MESH,
        )

    def layers(q, by):
        parts = []
        for bx in range(4):
            low = found[by * 4 + bx]
            high = found[16 + by * 4 + bx]
            near = recv[q][jnp.where(my_flip == 1, high, low)]
            far = recv[q][jnp.where(my_flip == 1, low, high)]
            parts.append(over(near, far))
        return jnp.stack(parts, axis=0)

    def share_out(q):
        for j in range(1, 4):
            by = (my_depth // 2 + j) % 4
            dsend[q, by] = layers(q, by)
            share(q, by).start()
        by = my_depth // 2
        mine = layers(q, by)

        @pl.when(my_depth % 2 == q // 2)
        def _():
            drecv[q % 2, my_depth] = mine

        @pl.when(my_depth % 2 != q // 2)
        def _():
            dsend[q, by] = mine
            share(q, by).start()

    def shared(q):
        for j in range(1, 4):
            share(q, (my_depth // 2 + j) % 4).wait_send()

        @pl.when(my_depth % 2 != q // 2)
        def _():
            share(q, my_depth // 2).wait_send()

    first(0).wait()
    set_fields(vox, mix, even, slopes, 0)
    first(1).wait()
    for q in range(QUARTERS):

        def group(m, carry, last=False):
            if q == 0:

                @pl.when(m + 1 < GROUPS)
                def _():
                    load(m + 1).wait()

            march(vox, img, mix, even, odd, slopes, sign, q, m, last)
            for o in range(N_TILE):
                image = img[pl.ds(rows[o], 8, stride=N_TILE), :]
                if o == 0:
                    recv[q][me * GROUPS + m] = image
                else:
                    send[q, o, m] = image
            if q == QUARTERS - 1:
                for o in range(1, N_TILE):
                    piece(m, o).start()
            return carry

        if q < QUARTERS - 1:
            lax.fori_loop(0, GROUPS, group, 0)
        else:
            lax.fori_loop(0, GROUPS - 1, group, 0)
            group(GROUPS - 1, 0, SPANS == 2)
        if q == 0:
            pl.semaphore_wait(barrier, N_TILE + N_DEPTH - 2)
        if q < QUARTERS - 1:
            for o in range(1, N_TILE):
                exchange(q, o).start()
        if q > 0:
            for o in range(1, N_TILE):
                exchange(q - 1, o).wait_recv()
            share_out(q - 1)
    for o in range(1, N_TILE):
        for q in range(QUARTERS - 1):
            exchange(q, o).wait_send()
    for q in range(QUARTERS - 1):
        shared(q)
    for m in range(GROUPS):
        for o in range(1, N_TILE):
            piece(m, o).wait_recv()
    share_out(QUARTERS - 1)
    for m in range(GROUPS):
        for o in range(1, N_TILE):
            piece(m, o).wait_send()

    def arrived(side, o):
        source = (my_depth + o) % N_DEPTH
        return pltpu.make_async_remote_copy(
            src_ref=dsend.at[side, 0],
            dst_ref=drecv.at[side, source],
            send_sem=dsend_sem.at[side, 0],
            recv_sem=drecv_sem.at[side, source],
            device_id={"depth": source},
            device_id_type=MESH,
        )

    for side in range(2):
        for o in range(1, N_DEPTH):
            arrived(side, o).wait_recv()
    lane_block = lax.broadcasted_iota(jnp.int32, (8, LANES), 1) // BLOCK
    for side in range(2):
        blended = [jnp.zeros((8, LANES), jnp.float32) for bx in range(4)]
        for i in range(N_DEPTH):
            level = jnp.where(my_flip == 1, i, N_DEPTH - 1 - i)
            layer = drecv[side, level]
            blended = [over(layer[bx], blended[bx]) for bx in range(4)]
        for y in range(4):
            line = blended[0]
            for bx in range(4):
                shift = (bx - y) * BLOCK % LANES
                moved = pltpu.roll(blended[bx], shift, 1) if shift else blended[bx]
                line = moved if bx == 0 else jnp.where(lane_block == bx, moved, line)
            for half in range(2):
                row = side * 8 + half * 4 + y
                out[pl.ds(row, 4, stride=16), :] = line[half * 4 : half * 4 + 4]
    shared(QUARTERS - 1)


def body(owned_blocks, slot_counts, brick_order, view_flip, tf_centers, tf_amps):
    smem = pl.BlockSpec(memory_space=pltpu.SMEM)
    image = pl.pallas_call(
        render,
        out_shape=jax.ShapeDtypeStruct((64, LANES), jnp.float32),
        in_specs=[smem] * 5 + [pl.BlockSpec(memory_space=pltpu.HBM)],
        out_specs=pl.BlockSpec(memory_space=pltpu.VMEM),
        scratch_shapes=[
            pltpu.VMEM((64, 32768), jnp.bfloat16),
            pltpu.VMEM((8 * N_TILE, LANES), jnp.float32),
            pltpu.VMEM((4 * HALF, KNOTS * HALF), jnp.float32),
            pltpu.VMEM((SPAN, 2, 4 * HALF, WIDE), jnp.float32),
            pltpu.VMEM((SPAN, 2, 4 * HALF, WIDE), jnp.float32),
            pltpu.VMEM((QUARTERS, N_TILE, GROUPS, 8, LANES), jnp.float32),
            pltpu.VMEM((N_TILE * GROUPS, 8, LANES), jnp.float32),
            pltpu.VMEM((N_TILE * GROUPS, 8, LANES), jnp.float32),
            pltpu.VMEM((N_TILE * GROUPS, 8, LANES), jnp.float32),
            pltpu.VMEM((N_TILE * GROUPS, 8, LANES), jnp.float32),
            pltpu.VMEM((QUARTERS, 4, 4, 8, LANES), jnp.float32),
            pltpu.VMEM((2, N_DEPTH, 4, 8, LANES), jnp.float32),
            pltpu.SMEM((N_TILE,), jnp.int32),
            pltpu.SMEM((N_TILE,), jnp.int32),
            pltpu.SMEM((2 * N_TILE,), jnp.int32),
            pltpu.SemaphoreType.DMA((GROUPS + 1,)),
            pltpu.SemaphoreType.DMA((QUARTERS - 1 + GROUPS, N_TILE)),
            pltpu.SemaphoreType.DMA((QUARTERS - 1 + GROUPS, N_TILE)),
            pltpu.SemaphoreType.DMA((QUARTERS, 4)),
            pltpu.SemaphoreType.DMA((2, N_DEPTH)),
        ],
        compiler_params=pltpu.CompilerParams(
            collective_id=0, has_side_effects=True, vmem_limit_bytes=64000 * 1024
        ),
        name="render",
    )(
        slot_counts.reshape(N_TILE),
        brick_order.reshape(N_TILE),
        view_flip,
        tf_centers,
        tf_amps,
        owned_blocks.reshape(64, 32768),
    )
    return image.reshape(4, 16, LANES)


def solution(mesh):
    in_specs = (P("depth", "tile", None), P("depth", None), P("depth", None), P(), P(), P())
    out_specs = P(None, "depth", "tile")
    return jax.shard_map(body, mesh=mesh, in_specs=in_specs, out_specs=out_specs, check_vma=False)
```

```python
import functools

import jax
import jax.numpy as jnp
from jax import lax
from jax.experimental import pallas as pl
from jax.experimental.pallas import tpu as pltpu
from jax.sharding import PartitionSpec as P

MESH = pl.DeviceIdType.MESH
BLOCK = 32
KNOTS = 8
N_TILE = 16
N_DEPTH = 8
GROUPS = 4
LANES = 128
PIXELS = BLOCK * BLOCK
STEP = 1.5 / 512
HALF = 8
WIDE = 256
LOG2E = 1.4426950408889634
SPAN = 16
JOIN = 4
SPANS = BLOCK // SPAN
QUARTERS = PIXELS // WIDE


def set_mix(mix, centers, amps):
    row = lax.broadcasted_iota(jnp.int32, (HALF, KNOTS * HALF), 0)
    column = lax.broadcasted_iota(jnp.int32, (HALF, KNOTS * HALF), 1)
    same = column % HALF == row
    block = column // HALF
    center = jnp.zeros(row.shape, jnp.float32)
    for k in range(KNOTS):
        center = jnp.where(block == k, centers[k], center)
    fall = jnp.exp(center * center * -4.0)
    for c in range(4):
        value = jnp.zeros(row.shape, jnp.float32)
        for k in range(KNOTS):
            value = jnp.where(block == k, amps[c][k], value)
        value = jnp.where(same, value * fall * (LOG2E if c == 3 else 0.5), 0.0)
        mix[c * HALF : (c + 1) * HALF, :] = value


def set_fields(vox, mix, fields, slopes, index):
    index = jnp.minimum(index, QUARTERS * GROUPS * SPANS - 1)
    row = pl.multiple_of(index // SPANS % GROUPS * N_TILE, N_TILE)
    first = index % SPANS * (SPAN * PIXELS) + index // (SPANS * GROUPS) * WIDE
    for start in range(0, SPAN, JOIN):
        halves = ([], [])
        for u in range(start, start + JOIN):
            lane = pl.multiple_of(first + u * PIXELS, WIDE)
            both = vox[pl.ds(row, N_TILE), pl.ds(lane, WIDE)].astype(jnp.float32)
            for h in range(2):
                value = both[h * HALF : (h + 1) * HALF]
                slope = value * (4.0 * LOG2E)
                bumps = [jnp.exp2(value * (s - slope)) for s in slopes]
                halves[h].append(jnp.concatenate(bumps, axis=0))
        for h in range(2):
            mixed = jnp.dot(
                mix[...],
                jnp.concatenate(halves[h], axis=1),
                preferred_element_type=jnp.float32,
                precision=lax.Precision.HIGH,
            )
            for u in range(JOIN):
                fields[start + u, h] = mixed[:, u * WIDE : (u + 1) * WIDE]


def advance(fields, step_sign, carry):
    for u in range(SPAN):
        total, held, red, green, blue = carry
        field = [
            jnp.concatenate([fields[u, h, c * HALF : (c + 1) * HALF] for h in range(2)], axis=0)
            for c in range(4)
        ]
        total = total + lax.log2(1.0 + jnp.exp2(field[3]))
        now = jnp.exp2(total * step_sign)
        weight = held - now
        red = red + weight * jnp.tanh(field[0])
        green = green + weight * jnp.tanh(field[1])
        blue = blue + weight * jnp.tanh(field[2])
        carry = total, now, red, green, blue
    return carry


def march(vox, img, mix, even, odd, slopes, sign, quarter, group, last):
    step_sign = sign * STEP
    base = (quarter * GROUPS + group) * SPANS

    def body(i, carry):
        set_fields(vox, mix, odd, slopes, base + 2 * i + 1)
        carry = advance(even, step_sign, carry)
        if not last:
            set_fields(vox, mix, even, slopes, base + 2 * i + 2)
        return advance(odd, step_sign, carry)

    zero = jnp.zeros((N_TILE, WIDE), jnp.float32)
    total, held, red, green, blue = lax.fori_loop(
        0, SPANS // 2, body, (zero, zero + 1.0, zero, zero, zero)
    )
    through = jnp.exp2(total * -STEP)
    scale = jnp.where(sign < 0.0, 0.5, -0.5 * through)
    values = [scale * ((1.0 - held) + colour) for colour in (red, green, blue)]
    values.append(1.0 - through)
    for c in range(4):
        for side in range(2):
            row = (side * 4 + c) * N_TILE
            img[row : row + N_TILE, :] = values[c][:, side * LANES : (side + 1) * LANES]


def neighbour(me, o):
    return (me // 4 + o // 4) % 4 * 4 + (me % 4 + o % 4) % 4


def hops(o):
    return min(o // 4, 4 - o // 4) + min(o % 4, 4 - o % 4)


FAR_FIRST = sorted(range(1, N_TILE), key=lambda o: -hops(o))


def over(nearer, farther):
    clear = 1.0 - nearer
    left = jnp.broadcast_to(clear[3:4], (4, LANES))
    right = jnp.broadcast_to(clear[7:8], (4, LANES))
    return nearer + jnp.concatenate([left, right], axis=0) * farther


def render(
    counts, order, flips, centers_ref, amps_ref, blocks, out,
    vox, img, mix, even, odd, send, recv0, recv1, recv2, recv3, dsend, drecv, starts, rows, found,
    load_sem, send_sem, recv_sem, dsend_sem, drecv_sem,
):
    me = lax.axis_index("tile")
    my_depth = lax.axis_index("depth")
    recv = (recv0, recv1, recv2, recv3)

    def load(m):
        part = pl.ds(pl.multiple_of(m * N_TILE, N_TILE), N_TILE)
        return pltpu.make_async_copy(blocks.at[part, :], vox.at[part, :], load_sem.at[m])

    def first(part):
        cells = pl.ds(part * SPAN * PIXELS, SPAN * PIXELS)
        rows_in = pl.ds(0, N_TILE)
        return pltpu.make_async_copy(
            blocks.at[rows_in, cells], vox.at[rows_in, cells], load_sem.at[part * GROUPS]
        )

    for part in range(2):
        first(part).start()
    for m in range(1, GROUPS):
        load(m).start()
    barrier = pltpu.get_barrier_semaphore()
    for o in range(1, N_TILE):
        pl.semaphore_signal(
            barrier, inc=1, device_id={"tile": neighbour(me, o)}, device_id_type=MESH
        )
    for o in range(1, N_DEPTH):
        pl.semaphore_signal(
            barrier, inc=1, device_id={"depth": (my_depth + o) % N_DEPTH}, device_id_type=MESH
        )

    running = jnp.int32(0)
    my_start = jnp.int32(0)
    my_position = jnp.int32(0)
    for i in range(N_TILE):
        starts[i] = running
        my_start = jnp.where(me == i, running, my_start)
        my_position = jnp.where(order[i] == me, i, my_position)
        running = running + counts[i]
    for o in range(N_TILE):
        tile = neighbour(me, o)
        position = jnp.int32(0)
        for i in range(N_TILE):
            position = jnp.where(order[i] == tile, i, position)
        rows[o] = (position - my_start) & (N_TILE - 1)

    def find(block, carry):
        for u in range(8):
            index = block * 8 + u
            wanted = index * N_TILE + my_position
            owner = jnp.int32(0)
            for hop in (8, 4, 2, 1):
                owner = jnp.where(starts[owner + hop] <= wanted, owner + hop, owner)
            depth = ((wanted - starts[owner]) >> 4) & (GROUPS - 1)
            found[index] = owner * GROUPS + depth
        return carry

    lax.fori_loop(0, N_TILE // 4, find, 0)
    my_flip = flips[me]
    slot = lax.broadcasted_iota(jnp.int32, (N_TILE, WIDE), 0)
    sign = jnp.full((N_TILE, WIDE), -1.0, jnp.float32)
    for s in range(N_TILE):
        flip = flips[order[(my_start + s) & (N_TILE - 1)]].astype(jnp.float32)
        sign = jnp.where(slot == s, 2.0 * flip - 1.0, sign)
    centers = [centers_ref[k] for k in range(KNOTS)]
    amps = [[amps_ref[c, k] for k in range(KNOTS)] for c in range(4)]
    set_mix(mix, centers, amps)
    slopes = [center * (8.0 * LOG2E) for center in centers]

    def exchange(q, o):
        return pltpu.make_async_remote_copy(
            src_ref=send.at[q, o],
            dst_ref=recv[q].at[pl.ds(me * GROUPS, GROUPS)],
            send_sem=send_sem.at[q, o],
            recv_sem=recv_sem.at[q, o],
            device_id={"tile": neighbour(me, o)},
            device_id_type=MESH,
        )

    def piece(m, o):
        return pltpu.make_async_remote_copy(
            src_ref=send.at[QUARTERS - 1, o, m],
            dst_ref=recv[QUARTERS - 1].at[me * GROUPS + m],
            send_sem=send_sem.at[QUARTERS - 1 + m, o],
            recv_sem=recv_sem.at[QUARTERS - 1 + m, o],
            device_id={"tile": neighbour(me, o)},
            device_id_type=MESH,
        )

    def share(q, by):
        return pltpu.make_async_remote_copy(
            src_ref=dsend.at[q, by],
            dst_ref=drecv.at[q % 2, my_depth],
            send_sem=dsend_sem.at[q, by],
            recv_sem=drecv_sem.at[q % 2, my_depth],
            device_id={"depth": 2 * by + q // 2},
            device_id_type=MESH,
        )

    def layers(q, by):
        parts = []
        for bx in range(4):
            low = found[by * 4 + bx]
            high = found[16 + by * 4 + bx]
            near = recv[q][jnp.where(my_flip == 1, high, low)]
            far = recv[q][jnp.where(my_flip == 1, low, high)]
            parts.append(over(near, far))
        return jnp.stack(parts, axis=0)

    def share_out(q):
        for j in (2, 1, 3):
            by = (my_depth // 2 + j) % 4
            dsend[q, by] = layers(q, by)
            share(q, by).start()
        by = my_depth // 2
        mine = layers(q, by)

        @pl.when(my_depth % 2 == q // 2)
        def _():
            drecv[q % 2, my_depth] = mine

        @pl.when(my_depth % 2 != q // 2)
        def _():
            dsend[q, by] = mine
            share(q, by).start()

    def shared(q):
        for j in range(1, 4):
            share(q, (my_depth // 2 + j) % 4).wait_send()

        @pl.when(my_depth % 2 != q // 2)
        def _():
            share(q, my_depth // 2).wait_send()

    first(0).wait()
    set_fields(vox, mix, even, slopes, 0)
    first(1).wait()
    for q in range(QUARTERS):

        def group(m, carry, last=False):
            if q == 0:

                @pl.when(m + 1 < GROUPS)
                def _():
                    load(m + 1).wait()

            march(vox, img, mix, even, odd, slopes, sign, q, m, last)
            for o in range(N_TILE):
                image = img[pl.ds(rows[o], 8, stride=N_TILE), :]
                if o == 0:
                    recv[q][me * GROUPS + m] = image
                else:
                    send[q, o, m] = image
            if q == QUARTERS - 1:
                for o in FAR_FIRST:
                    piece(m, o).start()
            return carry

        if q < QUARTERS - 1:
            lax.fori_loop(0, GROUPS, group, 0)
        else:
            lax.fori_loop(0, GROUPS - 1, group, 0)
            group(GROUPS - 1, 0, SPANS == 2)
        if q == 0:
            pl.semaphore_wait(barrier, N_TILE + N_DEPTH - 2)
        if q < QUARTERS - 1:
            for o in FAR_FIRST:
                exchange(q, o).start()
        if q > 0:
            for o in range(1, N_TILE):
                exchange(q - 1, o).wait_recv()
            share_out(q - 1)
    for o in range(1, N_TILE):
        for q in range(QUARTERS - 1):
            exchange(q, o).wait_send()
    for q in range(QUARTERS - 1):
        shared(q)
    for m in range(GROUPS):
        for o in range(1, N_TILE):
            piece(m, o).wait_recv()
    share_out(QUARTERS - 1)
    for m in range(GROUPS):
        for o in range(1, N_TILE):
            piece(m, o).wait_send()

    def arrived(side, o):
        source = (my_depth + o) % N_DEPTH
        return pltpu.make_async_remote_copy(
            src_ref=dsend.at[side, 0],
            dst_ref=drecv.at[side, source],
            send_sem=dsend_sem.at[side, 0],
            recv_sem=drecv_sem.at[side, source],
            device_id={"depth": source},
            device_id_type=MESH,
        )

    for side in range(2):
        for o in range(1, N_DEPTH):
            arrived(side, o).wait_recv()
    lane_block = lax.broadcasted_iota(jnp.int32, (8, LANES), 1) // BLOCK
    for side in range(2):
        blended = [jnp.zeros((8, LANES), jnp.float32) for bx in range(4)]
        for i in range(N_DEPTH):
            level = jnp.where(my_flip == 1, i, N_DEPTH - 1 - i)
            layer = drecv[side, level]
            blended = [over(layer[bx], blended[bx]) for bx in range(4)]
        for y in range(4):
            line = blended[0]
            for bx in range(4):
                shift = (bx - y) * BLOCK % LANES
                moved = pltpu.roll(blended[bx], shift, 1) if shift else blended[bx]
                line = moved if bx == 0 else jnp.where(lane_block == bx, moved, line)
            for half in range(2):
                row = side * 8 + half * 4 + y
                out[pl.ds(row, 4, stride=16), :] = line[half * 4 : half * 4 + 4]
    shared(QUARTERS - 1)


def body(owned_blocks, slot_counts, brick_order, view_flip, tf_centers, tf_amps):
    smem = pl.BlockSpec(memory_space=pltpu.SMEM)
    image = pl.pallas_call(
        render,
        out_shape=jax.ShapeDtypeStruct((64, LANES), jnp.float32),
        in_specs=[smem] * 5 + [pl.BlockSpec(memory_space=pltpu.HBM)],
        out_specs=pl.BlockSpec(memory_space=pltpu.VMEM),
        scratch_shapes=[
            pltpu.VMEM((64, 32768), jnp.bfloat16),
            pltpu.VMEM((8 * N_TILE, LANES), jnp.float32),
            pltpu.VMEM((4 * HALF, KNOTS * HALF), jnp.float32),
            pltpu.VMEM((SPAN, 2, 4 * HALF, WIDE), jnp.float32),
            pltpu.VMEM((SPAN, 2, 4 * HALF, WIDE), jnp.float32),
            pltpu.VMEM((QUARTERS, N_TILE, GROUPS, 8, LANES), jnp.float32),
            pltpu.VMEM((N_TILE * GROUPS, 8, LANES), jnp.float32),
            pltpu.VMEM((N_TILE * GROUPS, 8, LANES), jnp.float32),
            pltpu.VMEM((N_TILE * GROUPS, 8, LANES), jnp.float32),
            pltpu.VMEM((N_TILE * GROUPS, 8, LANES), jnp.float32),
            pltpu.VMEM((QUARTERS, 4, 4, 8, LANES), jnp.float32),
            pltpu.VMEM((2, N_DEPTH, 4, 8, LANES), jnp.float32),
            pltpu.SMEM((N_TILE,), jnp.int32),
            pltpu.SMEM((N_TILE,), jnp.int32),
            pltpu.SMEM((2 * N_TILE,), jnp.int32),
            pltpu.SemaphoreType.DMA((GROUPS + 1,)),
            pltpu.SemaphoreType.DMA((QUARTERS - 1 + GROUPS, N_TILE)),
            pltpu.SemaphoreType.DMA((QUARTERS - 1 + GROUPS, N_TILE)),
            pltpu.SemaphoreType.DMA((QUARTERS, 4)),
            pltpu.SemaphoreType.DMA((2, N_DEPTH)),
        ],
        compiler_params=pltpu.CompilerParams(
            collective_id=0, has_side_effects=True, vmem_limit_bytes=64000 * 1024
        ),
        name="render",
    )(
        slot_counts.reshape(N_TILE),
        brick_order.reshape(N_TILE),
        view_flip,
        tf_centers,
        tf_amps,
        owned_blocks.reshape(64, 32768),
    )
    return image.reshape(4, 16, LANES)


def solution(mesh):
    in_specs = (P("depth", "tile", None), P("depth", None), P("depth", None), P(), P(), P())
    out_specs = P(None, "depth", "tile")
    return jax.shard_map(body, mesh=mesh, in_specs=in_specs, out_specs=out_specs, check_vma=False)
```
